256 devices in a mesh: item: 32 (over x, z), day: 8 (over y, core).
Axes of the slice: x: 4, y: 4, z: 8, core: 2. Of those that a mesh axis runs over, the one named last changes fastest.
Arguments:
- user_factors: float32 [2048, 512], P(('item', 'day')), may hold values from 0.005 to 0.012
- item_factors: bfloat16 [16384, 512], P('item'), may hold values from 0 to 1
- day_factors: bfloat16 [368, 512], P('day'), may hold values from 0.099609375 to 1
- tile_counts: bfloat16 [32768, 128, 128], P(('item', 'day')), may hold values from 0 to 23
- tile_index: int32 [3, 32768], P(None, ('item', 'day')), may hold values from 0 to 45, as said below
- tile_live: int32 [256], P(('item', 'day')), may hold values from 32 to 128, as said below
Outputs:
- updated_users: float32 [2048, 512], P(('item', 'day'))
The draws below stay inside these ranges and needn't reach their ends.
Inputs may be any that keep to these rules, and one draw needn't show every extreme that they name: `tile_index`: row 0 names a user block below 16, row 1 an item block below 4 and row 2 a day below 46, local to the device that holds the slot. Only the first tile_live[d] slots of list d are live; some list has all 128 live.
All inputs are finite; a program needn't handle non-finite values.
Results may differ from the reference program's by a relative error of at most 0.003.
Values may be sent and summed in bfloat16 or wider, within the bound.
A program may use at most 64 MiB of HBM per device.

```python
import math
import jax
import jax.numpy as jnp
from jax import lax

R = 512
TILE = 128
GROUP = 8
CAP = 128
ITEMBLK_DEV = 4
DAY_DEV = 46
USERS = 2048
USER_BLOCKS = 16
ITEMS = 16384
DAYS = 368
DEVICE_SLOTS = 256
TILES_ALL = 32768
COUNT_SCALE = 23
N_ITEM = 32
N_DAY = 8


def draw_layout(key):
    first, second, third = jax.random.split(jax.random.fold_in(key, 11), 3)
    users = jax.random.randint(first, (TILES_ALL,), 0, USER_BLOCKS, dtype=jnp.int32)
    items = jax.random.randint(second, (TILES_ALL,), 0, ITEMBLK_DEV, dtype=jnp.int32)
    days = jax.random.randint(third, (TILES_ALL,), 0, DAY_DEV, dtype=jnp.int32)
    return jnp.stack([users, items, days], axis=0)


def log_even(key, shape, low, high):
    spread = jax.random.uniform(key, shape, jnp.float32, jnp.log(low), jnp.log(high))
    return jnp.exp(spread)


def sparse_rows(key, shape, base_low, base_high, big_low, big_high):
    first, second, third = jax.random.split(key, 3)
    base = log_even(first, shape, base_low, base_high)
    large = log_even(second, shape, big_low, big_high)
    chance = 8.0 / R
    picked = jax.random.bernoulli(third, chance, shape)
    return jnp.where(picked, large, base)


def draw_tile_index(key, part):
    return draw_layout(key)


def draw_tile_live(key, part):
    first, second = jax.random.split(jax.random.fold_in(key, 23), 2)
    counts = jax.random.randint(first, (DEVICE_SLOTS,), CAP // 4, CAP // 2 + 1, dtype=jnp.int32)
    fullest = jax.random.randint(second, (), 0, DEVICE_SLOTS, dtype=jnp.int32)
    return counts.at[fullest].set(CAP)


def draw_user_factors(key, part):
    inner = jax.random.fold_in(key, 31)
    values = log_even(inner, (USERS, R), 0.005, 0.012)
    return values


def draw_item_factors(key, part):
    return sparse_rows(jax.random.fold_in(key, 37), (ITEMS, R), 0.005, 0.015, 0.2, 1.0).astype(jnp.bfloat16)


def draw_tile_counts(key, part):
    layout = draw_layout(key)
    first, second, third = jax.random.split(jax.random.fold_in(key, 41), 3)
    user_level = log_even(first, (USERS,), 0.5, 2.0)
    item_level = log_even(second, (ITEMS,), 0.5, 2.0)
    noise = log_even(third, (TILES_ALL, TILE, TILE), 0.5, 2.0)
    slots = jnp.arange(TILES_ALL, dtype=jnp.int32)
    item_group = slots // CAP // N_DAY
    inside = jnp.arange(TILE, dtype=jnp.int32)
    user_ids = layout[0][:, None] * TILE + inside[None, :]
    item_ids = (item_group * ITEMBLK_DEV + layout[1])[:, None] * TILE + inside[None, :]
    levels = user_level[user_ids][:, :, None] * item_level[item_ids][:, None, :]
    counts = COUNT_SCALE * levels * noise / 8.0
    return counts.astype(jnp.bfloat16)


def block_scale(key, dims, cuts, least, largest):
    def one(dim, parts):
        draws = jax.random.uniform(jax.random.fold_in(jax.random.fold_in(key, 6), dim), (parts,), jnp.float32, least / len(cuts), largest / len(cuts))
        return jnp.repeat(jnp.exp(draws), dims[dim] // parts).reshape((-1,) + (1,) * (len(dims) - dim - 1))

    level = one(*cuts[0])
    for cut in cuts[1:]:
        level = level * one(*cut)
    return level


def setup_inputs(seed: int = 0) -> dict:
    key_of = jax.random.split(jax.random.key(seed), 7)
    user_factors = draw_user_factors(jax.random.fold_in(key_of[6], 71), 0)
    item_factors = draw_item_factors(jax.random.fold_in(key_of[6], 71), 0)
    day_factors = jnp.clip(jnp.exp(math.log(1.0) - 2.306499 * jax.random.uniform(key_of[2], (DAYS, R), jnp.float32) ** block_scale(key_of[2], (DAYS, R), ((0, 8),), -0.2, 0.2)), 0.099609375, 1.0).astype(jnp.bfloat16)
    tile_counts = draw_tile_counts(jax.random.fold_in(key_of[6], 71), 0)
    tile_index = draw_tile_index(jax.random.fold_in(key_of[6], 71), 0)
    tile_live = draw_tile_live(jax.random.fold_in(key_of[6], 71), 0)
    return {"user_factors": user_factors, "item_factors": item_factors, "day_factors": day_factors, "tile_counts": tile_counts, "tile_index": tile_index, "tile_live": tile_live}


def reference(user_factors, item_factors, day_factors, tile_counts, tile_index, tile_live):
    user_rows = user_factors.astype(jnp.bfloat16).reshape(USER_BLOCKS, TILE, R)
    item_blocks = item_factors.reshape(ITEMBLK_DEV * N_ITEM, TILE, R)
    slots = jnp.arange(TILES_ALL, dtype=jnp.int32)
    device = slots // CAP
    position = slots % CAP
    item_group = device // N_DAY
    day_group = device % N_DAY
    user_ids = tile_index[0]
    item_ids = item_group * ITEMBLK_DEV + tile_index[1]
    day_ids = day_group * DAY_DEV + tile_index[2]
    live = position < tile_live[device]
    turns = TILES_ALL // GROUP
    stacked = (tile_counts.reshape(turns, GROUP, TILE, TILE), user_ids.reshape(turns, GROUP),
               item_ids.reshape(turns, GROUP), day_ids.reshape(turns, GROUP), live.reshape(turns, GROUP))

    def turn(phi, pieces):
        counts, users, items, days, active = pieces
        scales = day_factors[days].astype(jnp.float32)[:, None, :]
        item_rows = item_blocks[items].astype(jnp.float32)
        scaled = (user_rows[users].astype(jnp.float32) * scales).astype(jnp.bfloat16)
        model = jnp.einsum("gur,gir->gui", scaled.astype(jnp.float32), item_rows)
        ratio = jnp.where(active[:, None, None], counts.astype(jnp.float32) / model, 0.0).astype(jnp.bfloat16)
        weighted = (item_rows * scales).astype(jnp.bfloat16)
        terms = jnp.einsum("gui,gir->gur", ratio.astype(jnp.float32), weighted.astype(jnp.float32))
        return phi.at[users].add(terms), None

    phi, _ = lax.scan(turn, jnp.zeros((USER_BLOCKS, TILE, R), jnp.float32), stacked)
    totals = jnp.sum(item_factors.astype(jnp.float32), axis=0) * jnp.sum(day_factors.astype(jnp.float32), axis=0)
    return user_factors * phi.reshape(USERS, R) / totals
```

```python
import functools

import jax
import jax.numpy as jnp
from jax import lax
from jax.experimental import pallas as pl
from jax.experimental.pallas import tpu as pltpu
from jax.sharding import PartitionSpec as P

MESH = pl.DeviceIdType.MESH
R = 512
TILE = 128
CAP = 128
USER_BLOCKS = 16
DAY_DEV = 46
ITEMBLK_DEV = 4
NX, NY, NZ, NC = 4, 4, 8, 2
ROWS = 8
FOUR = 4
ORDER = CAP + USER_BLOCKS * (FOUR - 1)


def place():
    item, day = lax.axis_index("item"), lax.axis_index("day")
    x, z = lax.div(item, NZ), lax.rem(item, NZ)
    y, c = lax.div(day, NC), lax.rem(day, NC)
    return x, y, z, c


def device(x, y, z, c):
    return (x * NZ + z, y * NC + c)


def pick(c, zero, one):
    return zero + c * (one - zero)


def along(first, me, step):
    x, y, z, c = me
    return device(
        pick(first, lax.rem(x + step, NX), x), pick(first, y, lax.rem(y + step, NY)), z, c
    )


def greet(me, c):
    x, y, z, _ = me
    barrier = pltpu.get_barrier_semaphore()
    for step in range(1, NZ):
        pl.semaphore_signal(
            barrier, inc=1, device_id=device(x, y, lax.rem(z + step, NZ), c), device_id_type=MESH
        )
    for step in range(1, NX):
        for first in (0, 1):
            pl.semaphore_signal(
                barrier, inc=1, device_id=along(first, me, step), device_id_type=MESH
            )
    pl.semaphore_signal(barrier, inc=1, device_id=device(x, y, z, 1 - c), device_id_type=MESH)
    pl.semaphore_wait(barrier, NZ - 1 + 2 * (NX - 1) + 1)


def send(src, dst, sems, spot, target):
    copy = pltpu.make_async_remote_copy(
        src_ref=src,
        dst_ref=dst,
        send_sem=sems[0].at[spot],
        recv_sem=sems[1].at[spot],
        device_id=target,
        device_id_type=MESH,
    )
    copy.start()
    return copy


def gather_kernel(
    user_ref, item_ref, day_ref, all_ref, total_ref,
    sums, sums_z, sums_a, sums_b, sums_c,
    z_s, z_r, a_s, a_r, b_s, b_r, c_s, c_r, tz_s, tz_r, ta_s, ta_r, tb_s, tb_r, tc_s, tc_r,
):
    me = place()
    x, y, z, c = me
    a, b = pick(c, x, y), pick(c, y, x)
    all_ref[c, a, b, z] = user_ref[...].astype(jnp.bfloat16)
    item_sum = jnp.sum(item_ref[...].astype(jnp.float32), axis=0, keepdims=True)
    day_sum = jnp.sum(day_ref[...].astype(jnp.float32), axis=0, keepdims=True)
    for part in range(R // 128):
        lanes = slice(part * 128, (part + 1) * 128)
        sums[part : part + 1, :] = item_sum[:, lanes]
        sums[part + 4 : part + 5, :] = day_sum[:, lanes]
    greet(me, c)

    copies = []
    spot = all_ref.at[c, a, b, z]
    for step in range(1, NZ):
        target = device(x, y, lax.rem(z + step, NZ), c)
        copies.append(send(spot, spot, (z_s, z_r), step - 1, target))
        copies.append(send(sums, sums_z.at[step - 1], (tz_s, tz_r), step - 1, target))
    for copy in copies:
        copy.wait()
    sums[...] += jnp.sum(sums_z[...], axis=0)

    copies = []
    spot = all_ref.at[c, a, b]
    for step in range(1, NX):
        target = along(c, me, step)
        copies.append(send(spot, spot, (a_s, a_r), step - 1, target))
        copies.append(send(sums, sums_a.at[step - 1], (ta_s, ta_r), step - 1, target))
    for copy in copies:
        copy.wait()
    sums[...] += jnp.sum(sums_a[...], axis=0)

    copies = []
    spot = all_ref.at[c, :, b]
    for step in range(1, NX):
        target = along(1 - c, me, step)
        copies.append(send(spot, spot, (b_s, b_r), step - 1, target))
        copies.append(send(sums, sums_b.at[step - 1], (tb_s, tb_r), step - 1, target))
    other = device(x, y, z, 1 - c)
    passed = [send(spot, spot, (c_s, c_r), 0, other)]
    for step in range(1, NX):
        arrived = all_ref.at[c, :, lax.rem(b - step + NX, NX)]
        copies[2 * step - 2].wait()
        passed.append(send(arrived, arrived, (c_s, c_r), step, other))
    for step in range(1, NX):
        copies[2 * step - 1].wait()
    sums[...] += jnp.sum(sums_b[...], axis=0)
    passed.append(send(sums, sums_c, (tc_s, tc_r), 0, other))
    for copy in passed:
        copy.wait()
    total_ref[...] = sums[...] + sums_c[...]


def gather_call(user_factors, item_factors, day_factors):
    dma = pltpu.SemaphoreType.DMA
    vmem = pl.BlockSpec(memory_space=pltpu.VMEM)
    tile = (8, 128)
    return pl.pallas_call(
        gather_kernel,
        out_shape=(
            jax.ShapeDtypeStruct((NC, NX, NY, NZ, ROWS, R), jnp.bfloat16),
            jax.ShapeDtypeStruct(tile, jnp.float32),
        ),
        in_specs=[vmem] * 3,
        out_specs=(vmem, vmem),
        scratch_shapes=[
            pltpu.VMEM(tile, jnp.float32),
            pltpu.VMEM((NZ - 1,) + tile, jnp.float32),
            pltpu.VMEM((NX - 1,) + tile, jnp.float32),
            pltpu.VMEM((NX - 1,) + tile, jnp.float32),
            pltpu.VMEM(tile, jnp.float32),
        ]
        + [dma((NZ - 1,))] * 2 + [dma((NX - 1,))] * 4 + [dma((NX,))] * 2
        + [dma((NZ - 1,))] * 2 + [dma((NX - 1,))] * 4 + [dma((1,))] * 2,
        compiler_params=pltpu.CompilerParams(collective_id=0, has_side_effects=True),
        name="gather_users",
    )(user_factors, item_factors, day_factors)


def phi_kernel(
    index_ref, live_ref, all_ref, item_ref, day_ref, counts_ref, phi_ref,
    users, scales, w_even, w_odd, m_even, m_odd, order, cursor, sem,
):
    copies = []
    for a in range(NX):
        for b in range(NX):
            for c in range(NC):
                x, y = (a, b) if c == 0 else (b, a)
                copies.append(
                    pltpu.make_async_copy(
                        all_ref.at[c, a, b],
                        users.at[pl.ds(x * NZ, NZ), pl.ds(y * NC * ROWS + c * ROWS, ROWS)],
                        sem.at[c, a, b],
                    )
                )
    for copy in copies:
        copy.start()
    live = live_ref[0]

    for block in range(USER_BLOCKS):
        cursor[block] = 0

    def count(slot, carry):
        block = index_ref[0, slot]
        cursor[block] = cursor[block] + 1
        return carry

    lax.fori_loop(0, live, count, 0)
    start = jnp.int32(0)
    for block in range(USER_BLOCKS):
        turns = lax.div(cursor[block] + (FOUR - 1), FOUR)
        cursor[block] = start
        start = start + turns * FOUR
    groups = lax.div(start, FOUR)

    def clear(spot, carry):
        order[spot] = -1
        return carry

    lax.fori_loop(0, start + 2 * FOUR, clear, 0)

    def put(slot, carry):
        block = index_ref[0, slot]
        spot = cursor[block]
        order[spot] = slot
        cursor[block] = spot + 1
        return carry

    lax.fori_loop(0, live, put, 0)

    day_rows = day_ref[...].astype(jnp.float32)
    for day in range(DAY_DEV):
        scales[day] = jnp.broadcast_to(day_rows[day : day + 1], (16, R)).astype(jnp.bfloat16)
    phi_ref[...] = jnp.zeros_like(phi_ref)
    for copy in copies:
        copy.wait()

    def slots(group):
        return [order[group * FOUR + part] for part in range(FOUR)]

    def forward(group, w, m):
        for part, slot in enumerate(slots(group)):
            slot = jnp.maximum(slot, 0)
            items = item_ref[index_ref[1, slot]].reshape(TILE // 16, 16, R)
            scaled = items * scales[index_ref[2, slot]][None]
            w[part * TILE : (part + 1) * TILE, :] = scaled.reshape(TILE, R)
        block = index_ref[0, jnp.maximum(order[group * FOUR], 0)]
        rows = users[pl.ds(2 * block, 2)].reshape(TILE, R)
        m[...] = lax.dot_general(
            rows, w[...], (((1,), (1,)), ((), ())), preferred_element_type=jnp.float32
        )

    def backward(group, w, m):
        ratios = []
        for part, slot in enumerate(slots(group)):
            tile = counts_ref[jnp.maximum(slot, 0)].astype(jnp.float32)
            ratio = tile / m[:, part * TILE : (part + 1) * TILE]
            ratios.append(jnp.where(slot >= 0, ratio, 0.0).astype(jnp.bfloat16))
        block = index_ref[0, jnp.maximum(order[group * FOUR], 0)]
        phi_ref[block] += jnp.dot(
            jnp.concatenate(ratios, axis=1), w[...], preferred_element_type=jnp.float32
        )

    forward(0, w_even, m_even)

    def turn(pair, carry):
        group = 2 * pair
        forward(group + 1, w_odd, m_odd)
        backward(group, w_even, m_even)
        forward(group + 2, w_even, m_even)
        backward(group + 1, w_odd, m_odd)
        return carry

    lax.fori_loop(0, lax.div(groups + 1, 2), turn, 0)


def phi_call(tile_index, tile_live, everyone, item_factors, day_factors, tile_counts):
    smem = pl.BlockSpec(memory_space=pltpu.SMEM)
    vmem = pl.BlockSpec(memory_space=pltpu.VMEM)
    w = pltpu.VMEM((FOUR * TILE, R), jnp.bfloat16)
    m = pltpu.VMEM((TILE, FOUR * TILE), jnp.float32)
    return pl.pallas_call(
        phi_kernel,
        out_shape=jax.ShapeDtypeStruct((USER_BLOCKS, TILE, R), jnp.float32),
        in_specs=[smem, smem, pl.BlockSpec(memory_space=pl.ANY), vmem, vmem, vmem],
        out_specs=vmem,
        scratch_shapes=[
            pltpu.VMEM((NX * NZ, NY * NC * ROWS, R), jnp.bfloat16),
            pltpu.VMEM((DAY_DEV, 16, R), jnp.bfloat16),
            w, w, m, m,
            pltpu.SMEM((ORDER + 4 * FOUR,), jnp.int32),
            pltpu.SMEM((USER_BLOCKS,), jnp.int32),
            pltpu.SemaphoreType.DMA((NC, NX, NX)),
        ],
        compiler_params=pltpu.CompilerParams(vmem_limit_bytes=40 << 20),
        name="tile_turns",
    )(tile_index, tile_live, everyone, item_factors, day_factors, tile_counts)


def scatter_kernel(
    phi_ref, user_ref, total_ref, out_ref,
    own, other, near, far, deep,
    own_sem, o_s, o_r, n_s, n_r, f_s, f_r, d_s, d_r,
):
    me = place()
    x, y, z, c = me
    p, q = pick(c, y, x), pick(c, x, y)
    pairs = [(kp, kq) for kq in (1, 2, 3, 0) for kp in (1, 2, 3, 0)]

    def mine(kp, kq):
        return lax.rem(p + kp, NX), lax.rem(q + kq, NX)

    locals_ = {}
    for kp, kq in pairs:
        pp, qq = mine(kp, kq)
        locals_[kp, kq] = pltpu.make_async_copy(
            phi_ref.at[pick(c, qq, pp), :, pick(c, pp, qq), c], own.at[kp, kq], own_sem.at[kp, kq]
        )
        locals_[kp, kq].start()
    greet(me, c)
    sibling = device(x, y, z, 1 - c)
    crossed = {}
    for kp, kq in pairs:
        pp, qq = lax.rem(q + kp, NX), lax.rem(p + kq, NX)
        src = phi_ref.at[pick(c, pp, qq), :, pick(c, qq, pp), 1 - c]
        crossed[kp, kq] = send(src, other.at[kp, kq], (o_s, o_r), (kp, kq), sibling)

    nears = {}
    fars = {}
    for kq in (1, 2, 3, 0):
        for kp in (1, 2, 3, 0):
            locals_[kp, kq].wait()
            crossed[kp, kq].wait()
            own[kp, kq] += other[kp, kq]
            if kp:
                nears[kp, kq] = send(
                    own.at[kp, kq], near.at[kp - 1, kq], (n_s, n_r), (kp - 1, kq),
                    along(1 - c, me, kp),
                )
    for kq in (1, 2, 3, 0):
        for kp in (1, 2, 3):
            nears[kp, kq].wait()
        own[0, kq] += near[0, kq] + near[1, kq] + near[2, kq]
        if kq:
            fars[kq] = send(
                own.at[0, kq], far.at[kq - 1], (f_s, f_r), kq - 1, along(c, me, kq)
            )
    for kq in (1, 2, 3):
        fars[kq].wait()
    own[0, 0] += far[0] + far[1] + far[2]
    deeps = []
    for step in range(1, NZ):
        there = lax.rem(z + step, NZ)
        deeps.append(
            send(own.at[0, 0, there], deep.at[step - 1], (d_s, d_r), step - 1,
                 device(x, y, there, c))
        )
    totals = total_ref[0:4, :] * total_ref[4:8, :] * (1.0 / (NX * NZ * NY * NC))
    for copy in deeps:
        copy.wait()
    summed = own[0, 0, z] + jnp.sum(deep[...], axis=0)
    for part in range(R // 128):
        lanes = slice(part * 128, (part + 1) * 128)
        out_ref[:, lanes] = user_ref[:, lanes] * summed[:, lanes] / totals[part : part + 1, :]


def scatter_call(phi, user_factors, totals):
    dma = pltpu.SemaphoreType.DMA
    vmem = pl.BlockSpec(memory_space=pltpu.VMEM)
    piece = (NZ, ROWS, R)
    return pl.pallas_call(
        scatter_kernel,
        out_shape=jax.ShapeDtypeStruct((ROWS, R), jnp.float32),
        in_specs=[pl.BlockSpec(memory_space=pl.ANY), vmem, vmem],
        out_specs=vmem,
        scratch_shapes=[
            pltpu.VMEM((NX, NX) + piece, jnp.float32),
            pltpu.VMEM((NX, NX) + piece, jnp.float32),
            pltpu.VMEM((NX - 1, NX) + piece, jnp.float32),
            pltpu.VMEM((NX - 1,) + piece, jnp.float32),
            pltpu.VMEM((NZ - 1, ROWS, R), jnp.float32),
            dma((NX, NX)), dma((NX, NX)), dma((NX, NX)),
            dma((NX - 1, NX)), dma((NX - 1, NX)),
            dma((NX - 1,)), dma((NX - 1,)),
            dma((NZ - 1,)), dma((NZ - 1,)),
        ],
        compiler_params=pltpu.CompilerParams(
            collective_id=1, has_side_effects=True, vmem_limit_bytes=24 << 20
        ),
        name="sum_phi",
    )(phi, user_factors, totals)


def per_device(user_factors, item_factors, day_factors, tile_counts, tile_index, tile_live):
    everyone, totals = gather_call(user_factors, item_factors, day_factors)
    phi = phi_call(
        tile_index, tile_live, everyone,
        item_factors.reshape(ITEMBLK_DEV, TILE, R), day_factors, tile_counts,
    )
    return scatter_call(phi.reshape(NX, NZ, NY, NC, ROWS, R), user_factors, totals)


def solution(mesh):
    in_specs = (
        P(("item", "day"), None),
        P("item", None),
        P("day", None),
        P(("item", "day"), None, None),
        P(None, ("item", "day")),
        P(("item", "day")),
    )
    out_specs = P(("item", "day"), None)
    return jax.shard_map(
        per_device, mesh=mesh, in_specs=in_specs, out_specs=out_specs, check_vma=False
    )
```

```python
import functools

import jax
import jax.numpy as jnp
from jax import lax
from jax.experimental import pallas as pl
from jax.experimental.pallas import tpu as pltpu
from jax.sharding import PartitionSpec as P

MESH = pl.DeviceIdType.MESH
R = 512
TILE = 128
CAP = 128
USER_BLOCKS = 16
DAY_DEV = 46
ITEMBLK_DEV = 4
NX, NY, NZ, NC = 4, 4, 8, 2
ROWS = 8
FOUR = 4
KEEP = 96
DAY_ROWS = 48


def place():
    item, day = lax.axis_index("item"), lax.axis_index("day")
    x, z = lax.div(item, NZ), lax.rem(item, NZ)
    y, c = lax.div(day, NC), lax.rem(day, NC)
    return x, y, z, c


def device(x, y, z, c):
    return (x * NZ + z, y * NC + c)


def pick(c, zero, one):
    return zero + c * (one - zero)


def along(first, me, step):
    x, y, z, c = me
    return device(
        pick(first, lax.rem(x + step, NX), x), pick(first, y, lax.rem(y + step, NY)), z, c
    )


def greet(me):
    x, y, z, c = me
    barrier = pltpu.get_barrier_semaphore()
    for step in range(1, NZ):
        pl.semaphore_signal(
            barrier, inc=1, device_id=device(x, y, lax.rem(z + step, NZ), c), device_id_type=MESH
        )
    for step in range(1, NX):
        for first in (0, 1):
            pl.semaphore_signal(
                barrier, inc=1, device_id=along(first, me, step), device_id_type=MESH
            )
    pl.semaphore_signal(barrier, inc=1, device_id=device(x, y, z, 1 - c), device_id_type=MESH)


def welcome():
    pl.semaphore_wait(pltpu.get_barrier_semaphore(), NZ - 1 + 2 * (NX - 1) + 1)


def send(src, dst, sems, spot, target):
    copy = pltpu.make_async_remote_copy(
        src_ref=src,
        dst_ref=dst,
        send_sem=sems[0].at[spot],
        recv_sem=sems[1].at[spot],
        device_id=target,
        device_id_type=MESH,
    )
    copy.start()
    return copy


def order_slots(mine, theirs):
    lane = lax.broadcasted_iota(jnp.int32, (1, CAP), 1)
    own = lane < KEEP
    users, items, days, live = (
        jnp.where(own, mine[row : row + 1], theirs[row : row + 1]) for row in range(4)
    )
    days = jnp.where(own, days, days + DAY_ROWS)
    code = 1 + lane + 128 * users + 2048 * items + 8192 * days
    users = jnp.where(lane < live, users, USER_BLOCKS)
    first = lax.broadcasted_iota(jnp.int32, (CAP, CAP), 0)
    second = lax.broadcasted_iota(jnp.int32, (CAP, CAP), 1)

    def column(row):
        return jnp.sum(jnp.where(first == second, row, 0), axis=1, keepdims=True)

    same = (column(users) == users) & (first < second)
    rank = jnp.sum(same.astype(jnp.int32), axis=0, keepdims=True)
    block = lax.broadcasted_iota(jnp.int32, (USER_BLOCKS, CAP), 0)
    sizes = jnp.sum((block == users).astype(jnp.int32), axis=1, keepdims=True)
    padded = lax.shift_left(lax.shift_right_logical(sizes + (FOUR - 1), 2), 2)
    before = jnp.sum(jnp.where(block < users, padded, 0), axis=0, keepdims=True)
    spot = column(jnp.where(users < USER_BLOCKS, before + rank, 2 * CAP))
    codes = column(code)
    rows = [
        jnp.sum(jnp.where(spot == second + half * CAP, codes, 0), axis=0, keepdims=True)
        for half in (0, 1)
    ]
    groups = jnp.sum(lax.shift_right_logical(padded, 2), axis=0, keepdims=True)
    return rows[0], rows[1], jnp.broadcast_to(groups, (1, CAP))


def gather_kernel(
    user_hbm, item_hbm, day_hbm, counts_hbm, index_hbm, live_ref,
    users, items, days, counts, plan, total_ref,
    user_ref, day_ref, index_ref, meta, meta_in, sums, sums_c, sums_b, sums_a, sums_z,
    local_sem, z_s, z_r, a_s, a_r, b_s, b_r, c_s, c_r, m_s, m_r,
    tc_s, tc_r, tb_s, tb_r, ta_s, ta_r, tz_s, tz_r,
):
    me = place()
    x, y, z, c = me
    load_user, load_index, load_day, load_items, load_counts = (
        pltpu.make_async_copy(src, dst, local_sem.at[spot])
        for spot, (src, dst) in enumerate((
            (user_hbm, user_ref), (index_hbm, index_ref), (day_hbm, day_ref),
            (item_hbm, items), (counts_hbm.at[pl.ds(0, KEEP)], counts.at[pl.ds(0, KEEP)]),
        ))
    )
    for copy in (load_user, load_index, load_day, load_items, load_counts):
        copy.start()
    greet(me)
    load_user.wait()
    users[x, z, y, c] = user_ref[...].astype(jnp.bfloat16)
    welcome()
    other = device(x, y, z, 1 - c)

    spot = users.at[x, z, y, c]
    along_z = [
        send(spot, spot, (z_s, z_r), step - 1, device(x, y, lax.rem(z + step, NZ), c))
        for step in range(1, NZ)
    ]
    load_index.wait()
    load_day.wait()
    days[DAY_ROWS - 8 : DAY_ROWS, :] = jnp.zeros((8, R), jnp.float32)
    days[0:DAY_DEV, :] = day_ref[...].astype(jnp.float32)
    meta[...] = jnp.zeros_like(meta)
    meta[0:3, :] = index_ref[...]
    meta[3:4, :] = jnp.full((1, CAP), live_ref[0], jnp.int32)
    swapped = [
        send(meta, meta_in, (m_s, m_r), 0, other),
        send(days.at[pl.ds(0, DAY_ROWS)], days.at[pl.ds(DAY_ROWS, DAY_ROWS)], (m_s, m_r), 1, other),
        send(
            counts_hbm.at[pl.ds(KEEP, CAP - KEEP)], counts.at[pl.ds(KEEP, CAP - KEEP)],
            (m_s, m_r), 2, other,
        ),
    ]
    load_items.wait()
    item_sum = jnp.sum(items[...].astype(jnp.float32), axis=0, keepdims=True)
    day_sum = jnp.sum(day_ref[...].astype(jnp.float32), axis=0, keepdims=True)
    for part in range(R // 128):
        lanes = slice(part * 128, (part + 1) * 128)
        sums[part : part + 1, :] = item_sum[:, lanes]
        sums[part + 4 : part + 5, :] = day_sum[:, lanes]
    add = send(sums, sums_c, (tc_s, tc_r), 0, other)
    add.wait()
    sums[...] += sums_c[...]
    adds = [
        send(sums, sums_b.at[step - 1], (tb_s, tb_r), step - 1, along(1 - c, me, step))
        for step in range(1, NX)
    ]

    for copy in along_z:
        copy.wait()
    spot = users.at[x, :, y, c]
    along_a = [
        send(spot, spot, (a_s, a_r), step - 1, along(c, me, step)) for step in range(1, NX)
    ]
    for copy in adds:
        copy.wait()
    sums[...] += jnp.sum(sums_b[...], axis=0)
    adds = [
        send(sums, sums_a.at[step - 1], (ta_s, ta_r), step - 1, along(c, me, step))
        for step in range(1, NX)
    ]

    for copy in along_a:
        copy.wait()
    along_b = {}
    passed = []
    for part in range(NX):
        spot = users.at[pick(c, part, x), :, pick(c, y, part), c]
        for step in (1, 3, 2):
            along_b[part, step] = send(
                spot, spot, (b_s, b_r), (step - 1, part), along(1 - c, me, step)
            )
        passed.append(send(spot, spot, (c_s, c_r), (0, part), other))
    for copy in adds:
        copy.wait()
    sums[...] += jnp.sum(sums_a[...], axis=0)
    adds = [
        send(sums, sums_z.at[step - 1], (tz_s, tz_r), step - 1, device(x, y, lax.rem(z + step, NZ), c))
        for step in range(1, NZ)
    ]
    swapped[0].wait()
    first, second, groups = order_slots(meta[...], meta_in[...])
    plan[0:1, :] = first
    plan[1:2, :] = second
    plan[2:3, :] = groups
    plan[3:8, :] = jnp.zeros((5, CAP), jnp.int32)

    for part in range(NX):
        for step in (1, 3, 2):
            along_b[part, step].wait()
            x_from, y_from = lax.rem(x - step + NX, NX), lax.rem(y - step + NY, NY)
            spot = users.at[pick(c, part, x_from), :, pick(c, y_from, part), c]
            passed.append(send(spot, spot, (c_s, c_r), (step, part), other))
    for copy in adds:
        copy.wait()
    total_ref[...] = sums[...] + jnp.sum(sums_z[...], axis=0)
    swapped[1].wait()
    swapped[2].wait()
    load_counts.wait()
    for copy in passed:
        copy.wait()


def gather_call(user_factors, item_factors, day_factors, tile_counts, tile_index, tile_live):
    dma = pltpu.SemaphoreType.DMA
    vmem = pl.BlockSpec(memory_space=pltpu.VMEM)
    hbm = pl.BlockSpec(memory_space=pltpu.HBM)
    tile = (8, 128)
    return pl.pallas_call(
        gather_kernel,
        out_shape=(
            pltpu.VMEM((NX, NZ, NY, NC, ROWS, R), jnp.bfloat16),
            pltpu.VMEM((ITEMBLK_DEV * TILE, R), jnp.bfloat16),
            pltpu.VMEM((2 * DAY_ROWS, R), jnp.float32),
            pltpu.VMEM((CAP, TILE, TILE), jnp.bfloat16),
            pltpu.VMEM(tile, jnp.int32),
            pltpu.VMEM(tile, jnp.float32),
        ),
        in_specs=[hbm] * 5 + [pl.BlockSpec(memory_space=pltpu.SMEM)],
        out_specs=(vmem,) * 6,
        scratch_shapes=[
            pltpu.VMEM((ROWS, R), jnp.float32),
            pltpu.VMEM((DAY_DEV, R), jnp.bfloat16),
            pltpu.VMEM((3, CAP), jnp.int32),
            pltpu.VMEM(tile, jnp.int32),
            pltpu.VMEM(tile, jnp.int32),
            pltpu.VMEM(tile, jnp.float32),
            pltpu.VMEM(tile, jnp.float32),
            pltpu.VMEM((NX - 1,) + tile, jnp.float32),
            pltpu.VMEM((NX - 1,) + tile, jnp.float32),
            pltpu.VMEM((NZ - 1,) + tile, jnp.float32),
            dma((5,)),
        ]
        + [dma((NZ - 1,))] * 2 + [dma((NX - 1,))] * 2 + [dma((NX - 1, NX))] * 2
        + [dma((NX, NX))] * 2 + [dma((3,))] * 2
        + [dma((1,))] * 2 + [dma((NX - 1,))] * 4 + [dma((NZ - 1,))] * 2,
        compiler_params=pltpu.CompilerParams(
            collective_id=0, has_side_effects=True, vmem_limit_bytes=8 << 20
        ),
        name="gather_users",
    )(user_factors, item_factors, day_factors, tile_counts, tile_index, tile_live)


def phi_kernel(
    plan_ref, users_ref, item_ref, day_ref, counts_ref, phi_ref, w_even, w_odd, m_even, m_odd
):
    phi_ref[...] = jnp.zeros_like(phi_ref)
    groups = plan_ref[2, 0]

    def codes(group):
        spot = FOUR * group
        row, col = lax.shift_right_logical(spot, 7), spot & (CAP - 1)
        return [plan_ref[row, col + part] for part in range(FOUR)]

    def user_block(code):
        return lax.shift_right_logical(jnp.maximum(code - 1, 0), 7) & (USER_BLOCKS - 1)

    def forward(group, w, m):
        group_codes = codes(group)
        for part, code in enumerate(group_codes):
            code = jnp.maximum(code - 1, 0)
            items = item_ref[lax.shift_right_logical(code, 11) & 3]
            scale = day_ref[pl.ds(lax.shift_right_logical(code, 13), 1), :]
            scale = jnp.broadcast_to(scale, (16, R)).astype(jnp.bfloat16)
            scaled = items.reshape(TILE // 16, 16, R) * scale[None]
            w[part * TILE : (part + 1) * TILE, :] = scaled.reshape(TILE, R)
        m[...] = lax.dot_general(
            users_ref[user_block(group_codes[0])], w[...], (((1,), (1,)), ((), ())),
            preferred_element_type=jnp.float32,
        )

    def backward(group, w, m):
        group_codes = codes(group)
        ratios = []
        for part, code in enumerate(group_codes):
            tile = counts_ref[jnp.maximum(code - 1, 0) & (CAP - 1)].astype(jnp.float32)
            ratio = tile / m[:, part * TILE : (part + 1) * TILE]
            ratios.append(jnp.where(code > 0, ratio, 0.0).astype(jnp.bfloat16))
        phi_ref[user_block(group_codes[0])] += jnp.dot(
            jnp.concatenate(ratios, axis=1), w[...], preferred_element_type=jnp.float32
        )

    forward(0, w_even, m_even)

    def turn(pair, carry):
        group = 2 * pair
        forward(group + 1, w_odd, m_odd)
        backward(group, w_even, m_even)
        forward(group + 2, w_even, m_even)
        backward(group + 1, w_odd, m_odd)
        return carry

    lax.fori_loop(0, lax.shift_right_logical(groups + 1, 1), turn, 0)


def phi_call(plan, users, items, days, counts):
    vmem = pl.BlockSpec(memory_space=pltpu.VMEM)
    w = pltpu.VMEM((FOUR * TILE, R), jnp.bfloat16)
    m = pltpu.VMEM((TILE, FOUR * TILE), jnp.float32)
    return pl.pallas_call(
        phi_kernel,
        out_shape=pltpu.VMEM((USER_BLOCKS, TILE, R), jnp.float32),
        in_specs=[pl.BlockSpec(memory_space=pltpu.SMEM)] + [vmem] * 4,
        out_specs=vmem,
        scratch_shapes=[w, w, m, m],
        compiler_params=pltpu.CompilerParams(vmem_limit_bytes=32 << 20),
        name="tile_turns",
    )(plan, users, items, days, counts)


def scatter_kernel(
    phi_ref, user_ref, total_ref, out_ref,
    other, out_near, near, kept, far, deep,
    o_s, o_r, n_s, n_r, f_s, f_r, d_s, d_r,
):
    me = place()
    x, y, z, c = me
    p, q = pick(c, y, x), pick(c, x, y)
    greet(me)
    welcome()
    sibling = device(x, y, z, 1 - c)
    pairs = [(kp, kq) for kq in (1, 2, 3, 0) for kp in (1, 2, 3, 0)]
    crossed = {}
    for kp, kq in pairs:
        pp, qq = lax.rem(q + kp, NX), lax.rem(p + kq, NX)
        src = phi_ref.at[pick(c, pp, qq), :, pick(c, qq, pp), 1 - c]
        crossed[kp, kq] = send(src, other.at[kp, kq], (o_s, o_r), (kp, kq), sibling)

    nears, fars = {}, {}
    for kp, kq in pairs:
        pp, qq = lax.rem(p + kp, NX), lax.rem(q + kq, NX)
        crossed[kp, kq].wait()
        piece = phi_ref[pick(c, qq, pp), :, pick(c, pp, qq), c] + other[kp, kq]
        if kp:
            out_near[kp - 1, kq] = piece.reshape(NZ * ROWS, R).astype(jnp.bfloat16)
            nears[kp, kq] = send(
                out_near.at[kp - 1, kq], near.at[kp - 1, kq], (n_s, n_r), (kp - 1, kq),
                along(1 - c, me, kp),
            )
        else:
            kept[kq] = piece
    for kq in (1, 2, 3, 0):
        piece = kept[kq]
        for kp in (1, 2, 3):
            nears[kp, kq].wait()
            piece += near[kp - 1, kq].astype(jnp.float32).reshape(NZ, ROWS, R)
        kept[kq] = piece
        if kq:
            fars[kq] = send(kept.at[kq], far.at[kq - 1], (f_s, f_r), kq - 1, along(c, me, kq))
    for kq in (1, 2, 3):
        fars[kq].wait()
    kept[0] += far[0] + far[1] + far[2]
    deeps = []
    for step in range(1, NZ):
        there = lax.rem(z + step, NZ)
        deeps.append(
            send(kept.at[0, there], deep.at[step - 1], (d_s, d_r), step - 1,
                 device(x, y, there, c))
        )
    totals = total_ref[0:4, :] * total_ref[4:8, :] * (1.0 / (NX * NZ * NY * NC))
    for copy in deeps:
        copy.wait()
    summed = kept[0, z] + jnp.sum(deep[...], axis=0)
    for part in range(R // 128):
        lanes = slice(part * 128, (part + 1) * 128)
        out_ref[:, lanes] = user_ref[:, lanes] * summed[:, lanes] / totals[part : part + 1, :]


def scatter_call(phi, user_factors, totals):
    dma = pltpu.SemaphoreType.DMA
    vmem = pl.BlockSpec(memory_space=pltpu.VMEM)
    piece = (NZ, ROWS, R)
    return pl.pallas_call(
        scatter_kernel,
        out_shape=jax.ShapeDtypeStruct((ROWS, R), jnp.float32),
        in_specs=[vmem] * 3,
        out_specs=vmem,
        scratch_shapes=[
            pltpu.VMEM((NX, NX) + piece, jnp.float32),
            pltpu.VMEM((NX - 1, NX, NZ * ROWS, R), jnp.bfloat16),
            pltpu.VMEM((NX - 1, NX, NZ * ROWS, R), jnp.bfloat16),
            pltpu.VMEM((NX,) + piece, jnp.float32),
            pltpu.VMEM((NX - 1,) + piece, jnp.float32),
            pltpu.VMEM((NZ - 1, ROWS, R), jnp.float32),
            dma((NX, NX)), dma((NX, NX)),
            dma((NX - 1, NX)), dma((NX - 1, NX)),
            dma((NX - 1,)), dma((NX - 1,)),
            dma((NZ - 1,)), dma((NZ - 1,)),
        ],
        compiler_params=pltpu.CompilerParams(
            collective_id=1, has_side_effects=True, vmem_limit_bytes=24 << 20
        ),
        name="sum_phi",
    )(phi, user_factors, totals)


def per_device(user_factors, item_factors, day_factors, tile_counts, tile_index, tile_live):
    in_hbm = functools.partial(pltpu.with_memory_space_constraint, memory_space=pltpu.HBM)
    users, items, days, counts, plan, totals = gather_call(
        *map(in_hbm, (user_factors, item_factors, day_factors, tile_counts, tile_index)), tile_live
    )
    phi = phi_call(
        plan, users.reshape(USER_BLOCKS, TILE, R), items.reshape(ITEMBLK_DEV, TILE, R), days, counts
    )
    return scatter_call(phi.reshape(NX, NZ, NY, NC, ROWS, R), user_factors, totals)


def solution(mesh):
    in_specs = (
        P(("item", "day"), None),
        P("item", None),
        P("day", None),
        P(("item", "day"), None, None),
        P(None, ("item", "day")),
        P(("item", "day")),
    )
    out_specs = P(("item", "day"), None)
    return jax.shard_map(
        per_device, mesh=mesh, in_specs=in_specs, out_specs=out_specs, check_vma=False
    )
```

```python
import functools

import jax
import jax.numpy as jnp
from jax import lax
from jax.experimental import pallas as pl
from jax.experimental.pallas import tpu as pltpu
from jax.sharding import PartitionSpec as P

MESH = pl.DeviceIdType.MESH
R = 512
TILE = 128
CAP = 128
USER_BLOCKS = 16
DAY_DEV = 46
ITEMBLK_DEV = 4
NX, NY, NZ, NC = 4, 4, 8, 2
ROWS = 8
FOUR = 4
KEEP = 96
DAY_ROWS = 48
STEPS = (2, 1, 3, 0)
SHARES = (pl.ds(0, 5), pl.ds(5, 3))


def place():
    item, day = lax.axis_index("item"), lax.axis_index("day")
    x, z = lax.div(item, NZ), lax.rem(item, NZ)
    y, c = lax.div(day, NC), lax.rem(day, NC)
    return x, y, z, c


def device(x, y, z, c):
    return (x * NZ + z, y * NC + c)


def pick(c, zero, one):
    return zero + c * (one - zero)


def along(first, me, step):
    x, y, z, c = me
    return device(
        pick(first, lax.rem(x + step, NX), x), pick(first, y, lax.rem(y + step, NY)), z, c
    )


def z_place(ahead):
    return (0, 1, 3, 5, 7, 6, 4, 2)[ahead]


def greet(me):
    x, y, z, c = me
    barrier = pltpu.get_barrier_semaphore()
    for step in range(1, NZ):
        pl.semaphore_signal(
            barrier, inc=1, device_id=device(x, y, lax.rem(z + step, NZ), c), device_id_type=MESH
        )
    for step in range(1, NX):
        for first in (0, 1):
            pl.semaphore_signal(
                barrier, inc=1, device_id=along(first, me, step), device_id_type=MESH
            )
    pl.semaphore_signal(barrier, inc=1, device_id=device(x, y, z, 1 - c), device_id_type=MESH)


def welcome():
    pl.semaphore_wait(pltpu.get_barrier_semaphore(), NZ - 1 + 2 * (NX - 1) + 1)


def send(src, dst, sems, spot, target):
    copy = pltpu.make_async_remote_copy(
        src_ref=src,
        dst_ref=dst,
        send_sem=sems[0].at[spot],
        recv_sem=sems[1].at[spot],
        device_id=target,
        device_id_type=MESH,
    )
    copy.start()
    return copy


def order_slots(mine, theirs):
    lane = lax.broadcasted_iota(jnp.int32, (1, CAP), 1)
    own = lane < KEEP
    users, items, days, live = (
        jnp.where(own, mine[row : row + 1], theirs[row : row + 1]) for row in range(4)
    )
    days = jnp.where(own, days, days + DAY_ROWS)
    code = 1 + lane + 128 * users + 2048 * items + 8192 * days
    users = jnp.where(lane < live, users, USER_BLOCKS)
    first = lax.broadcasted_iota(jnp.int32, (CAP, CAP), 0)
    second = lax.broadcasted_iota(jnp.int32, (CAP, CAP), 1)

    def column(row):
        return jnp.sum(jnp.where(first == second, row, 0), axis=1, keepdims=True)

    same = (column(users) == users) & (first < second)
    rank = jnp.sum(same.astype(jnp.int32), axis=0, keepdims=True)
    block = lax.broadcasted_iota(jnp.int32, (USER_BLOCKS, CAP), 0)
    sizes = jnp.sum((block == users).astype(jnp.int32), axis=1, keepdims=True)
    padded = lax.shift_left(lax.shift_right_logical(sizes + (FOUR - 1), 2), 2)
    before = jnp.sum(jnp.where(block < users, padded, 0), axis=0, keepdims=True)
    spot = column(jnp.where(users < USER_BLOCKS, before + rank, 2 * CAP))
    codes = column(code)
    rows = [
        jnp.sum(jnp.where(spot == second + half * CAP, codes, 0), axis=0, keepdims=True)
        for half in (0, 1)
    ]
    groups = jnp.sum(lax.shift_right_logical(padded, 2), axis=0, keepdims=True)
    return rows[0], rows[1], jnp.broadcast_to(groups, (1, CAP))


def gather_kernel(
    user_hbm, item_hbm, day_hbm, counts_hbm, index_hbm, live_ref,
    users, items, days, counts, plan, total_ref,
    user_ref, day_ref, index_ref, meta, meta_in, sums, sums_c, sums_b, sums_a, sums_z,
    local_sem, z_s, z_r, a_s, a_r, b_s, b_r, c_s, c_r, m_s, m_r,
    tc_s, tc_r, tb_s, tb_r, ta_s, ta_r, tz_s, tz_r,
):
    me = place()
    x, y, z, c = me
    load_user, load_index, load_day, load_items, load_counts = (
        pltpu.make_async_copy(src, dst, local_sem.at[spot])
        for spot, (src, dst) in enumerate((
            (user_hbm, user_ref), (index_hbm, index_ref), (day_hbm, day_ref),
            (item_hbm, items), (counts_hbm.at[pl.ds(0, KEEP)], counts.at[pl.ds(0, KEEP)]),
        ))
    )
    for copy in (load_user, load_index, load_day, load_items, load_counts):
        copy.start()
    greet(me)
    load_user.wait()
    users[x, 0, y, c] = user_ref[...].astype(jnp.bfloat16)
    welcome()
    other = device(x, y, z, 1 - c)

    a, b = pick(c, x, y), pick(c, y, x)

    def piece(back_a, back_b, share):
        a_from, b_from = lax.rem(a - back_a + NX, NX), lax.rem(b - back_b + NX, NX)
        return users.at[pick(c, a_from, b_from), SHARES[share], pick(c, b_from, a_from), c]

    def forward(back_a, share):
        spot = piece(back_a, 0, share)
        for step in (2, 1, 3):
            along_b[step, back_a, share] = send(
                spot, spot, (b_s, b_r), (step - 1, back_a, share), along(1 - c, me, step)
            )
        cross(back_a, 0, share)

    def cross(back_a, back_b, share):
        spot = piece(back_a, back_b, share)
        passed.append(send(spot, spot, (c_s, c_r), (back_a, back_b, share), other))

    def spread(share):
        spot = piece(0, 0, share)
        for step in (2, 1, 3):
            along_a[step, share] = send(
                spot, spot, (a_s, a_r), (step - 1, share), along(c, me, step)
            )
        forward(0, share)

    along_a, along_b, passed = {}, {}, []
    along_z = {
        step: send(
            users.at[x, 0, y, c], users.at[x, z_place(NZ - step), y, c], (z_s, z_r), step - 1,
            device(x, y, lax.rem(z + step, NZ), c),
        )
        for step in (2, 6, 1, 7, 4, 3, 5)
    }
    load_index.wait()
    load_day.wait()
    days[0:DAY_DEV, :] = day_ref[...].astype(jnp.float32)
    days[DAY_DEV:DAY_ROWS, :] = jnp.zeros((DAY_ROWS - DAY_DEV, R), jnp.float32)
    meta[...] = jnp.zeros_like(meta)
    meta[0:3, :] = index_ref[...]
    meta[3:4, :] = jnp.full((1, CAP), live_ref[0], jnp.int32)
    swapped = [
        send(meta, meta_in, (m_s, m_r), 0, other),
        send(days.at[pl.ds(0, DAY_ROWS)], days.at[pl.ds(DAY_ROWS, DAY_ROWS)], (m_s, m_r), 1, other),
        send(
            counts_hbm.at[pl.ds(KEEP, CAP - KEEP)], counts.at[pl.ds(KEEP, CAP - KEEP)],
            (m_s, m_r), 2, other,
        ),
    ]
    load_items.wait()
    item_sum = jnp.sum(items[...].astype(jnp.float32), axis=0, keepdims=True)
    day_sum = jnp.sum(day_ref[...].astype(jnp.float32), axis=0, keepdims=True)
    for part in range(R // 128):
        lanes = slice(part * 128, (part + 1) * 128)
        sums[part : part + 1, :] = item_sum[:, lanes]
        sums[part + 4 : part + 5, :] = day_sum[:, lanes]
    add = send(sums, sums_c, (tc_s, tc_r), 0, other)

    for step in (7, 1, 6, 2):
        along_z[step].wait()
    spread(0)
    add.wait()
    sums[...] += sums_c[...]
    adds = [
        send(sums, sums_b.at[step - 1], (tb_s, tb_r), step - 1, along(1 - c, me, step))
        for step in range(1, NX)
    ]
    for step in (5, 3, 4):
        along_z[step].wait()
    spread(1)
    for copy in adds:
        copy.wait()
    sums[...] += jnp.sum(sums_b[...], axis=0)
    adds = [
        send(sums, sums_a.at[step - 1], (ta_s, ta_r), step - 1, along(c, me, step))
        for step in range(1, NX)
    ]
    for share in (0, 1):
        for step in (1, 3, 2):
            along_a[step, share].wait()
            forward(step, share)
    for copy in adds:
        copy.wait()
    sums[...] += jnp.sum(sums_a[...], axis=0)
    adds = [
        send(sums, sums_z.at[step - 1], (tz_s, tz_r), step - 1, device(x, y, lax.rem(z + step, NZ), c))
        for step in range(1, NZ)
    ]
    swapped[0].wait()
    first, second, groups = order_slots(meta[...], meta_in[...])
    plan[0:1, :] = first
    plan[1:2, :] = second
    plan[2:3, :] = groups
    plan[3:4, :] = jnp.full((1, CAP), z, jnp.int32)
    plan[4:8, :] = jnp.zeros((4, CAP), jnp.int32)

    for back_a, share in ((0, 0), (0, 1), (1, 0), (3, 0), (2, 0), (1, 1), (3, 1), (2, 1)):
        for step in (1, 3, 2):
            along_b[step, back_a, share].wait()
            cross(back_a, step, share)
    for copy in adds:
        copy.wait()
    total_ref[...] = sums[...] + jnp.sum(sums_z[...], axis=0)
    swapped[1].wait()
    swapped[2].wait()
    load_counts.wait()
    for copy in passed:
        copy.wait()


def gather_call(user_factors, item_factors, day_factors, tile_counts, tile_index, tile_live):
    dma = pltpu.SemaphoreType.DMA
    vmem = pl.BlockSpec(memory_space=pltpu.VMEM)
    hbm = pl.BlockSpec(memory_space=pltpu.HBM)
    tile = (8, 128)
    return pl.pallas_call(
        gather_kernel,
        out_shape=(
            pltpu.VMEM((NX, NZ, NY, NC, ROWS, R), jnp.bfloat16),
            pltpu.VMEM((ITEMBLK_DEV * TILE, R), jnp.bfloat16),
            pltpu.VMEM((2 * DAY_ROWS, R), jnp.float32),
            pltpu.VMEM((CAP, TILE, TILE), jnp.bfloat16),
            pltpu.VMEM(tile, jnp.int32),
            pltpu.VMEM(tile, jnp.float32),
        ),
        in_specs=[hbm] * 5 + [pl.BlockSpec(memory_space=pltpu.SMEM)],
        out_specs=(vmem,) * 6,
        scratch_shapes=[
            pltpu.VMEM((ROWS, R), jnp.float32),
            pltpu.VMEM((DAY_DEV, R), jnp.bfloat16),
            pltpu.VMEM((3, CAP), jnp.int32),
            pltpu.VMEM(tile, jnp.int32),
            pltpu.VMEM(tile, jnp.int32),
            pltpu.VMEM(tile, jnp.float32),
            pltpu.VMEM(tile, jnp.float32),
            pltpu.VMEM((NX - 1,) + tile, jnp.float32),
            pltpu.VMEM((NX - 1,) + tile, jnp.float32),
            pltpu.VMEM((NZ - 1,) + tile, jnp.float32),
            dma((5,)),
        ]
        + [dma((NZ - 1,))] * 2 + [dma((NX - 1, 2))] * 2 + [dma((NX - 1, NX, 2))] * 2
        + [dma((NX, NX, 2))] * 2 + [dma((3,))] * 2
        + [dma((1,))] * 2 + [dma((NX - 1,))] * 4 + [dma((NZ - 1,))] * 2,
        compiler_params=pltpu.CompilerParams(
            collective_id=0, has_side_effects=True, vmem_limit_bytes=8 << 20
        ),
        name="gather_users",
    )(user_factors, item_factors, day_factors, tile_counts, tile_index, tile_live)


def phi_kernel(
    plan_ref, users_ref, item_ref, day_ref, counts_ref, phi_ref, w_even, w_odd, m_even, m_odd
):
    phi_ref[...] = jnp.zeros_like(phi_ref)
    groups, z = plan_ref[2, 0], plan_ref[3, 0]

    def user_rows(block):
        halves = []
        for half in (0, 1):
            ahead = (2 * (block & 3) + half - z) & (NZ - 1)
            spot = jnp.where(ahead <= NZ // 2, jnp.maximum(2 * ahead - 1, 0), 2 * (NZ - ahead))
            halves.append(users_ref[lax.shift_right_logical(block, 2) * NZ + spot])
        return jnp.concatenate(halves, axis=0)

    def codes(group):
        spot = FOUR * group
        row, col = lax.shift_right_logical(spot, 7), spot & (CAP - 1)
        return [plan_ref[row, col + part] for part in range(FOUR)]

    def user_block(code):
        return lax.shift_right_logical(jnp.maximum(code - 1, 0), 7) & (USER_BLOCKS - 1)

    def forward(group, w, m):
        group_codes = codes(group)
        for part, code in enumerate(group_codes):
            code = jnp.maximum(code - 1, 0)
            items = item_ref[lax.shift_right_logical(code, 11) & 3]
            scale = day_ref[pl.ds(lax.shift_right_logical(code, 13), 1), :]
            scale = jnp.broadcast_to(scale, (16, R)).astype(jnp.bfloat16)
            scaled = items.reshape(TILE // 16, 16, R) * scale[None]
            w[part * TILE : (part + 1) * TILE, :] = scaled.reshape(TILE, R)
        m[...] = lax.dot_general(
            user_rows(user_block(group_codes[0])), w[...], (((1,), (1,)), ((), ())),
            preferred_element_type=jnp.float32,
        )

    def backward(group, w, m):
        group_codes = codes(group)
        ratios = []
        for part, code in enumerate(group_codes):
            tile = counts_ref[jnp.maximum(code - 1, 0) & (CAP - 1)].astype(jnp.float32)
            ratio = tile / m[:, part * TILE : (part + 1) * TILE]
            ratios.append(jnp.where(code > 0, ratio, 0.0).astype(jnp.bfloat16))
        phi_ref[user_block(group_codes[0])] += jnp.dot(
            jnp.concatenate(ratios, axis=1), w[...], preferred_element_type=jnp.float32
        )

    forward(0, w_even, m_even)

    def turn(pair, carry):
        group = 2 * pair
        forward(group + 1, w_odd, m_odd)
        backward(group, w_even, m_even)
        forward(group + 2, w_even, m_even)
        backward(group + 1, w_odd, m_odd)
        return carry

    lax.fori_loop(0, lax.shift_right_logical(groups + 1, 1), turn, 0)


def phi_call(plan, users, items, days, counts):
    vmem = pl.BlockSpec(memory_space=pltpu.VMEM)
    w = pltpu.VMEM((FOUR * TILE, R), jnp.bfloat16)
    m = pltpu.VMEM((TILE, FOUR * TILE), jnp.float32)
    return pl.pallas_call(
        phi_kernel,
        out_shape=pltpu.VMEM((USER_BLOCKS, TILE, R), jnp.float32),
        in_specs=[pl.BlockSpec(memory_space=pltpu.SMEM)] + [vmem] * 4,
        out_specs=vmem,
        scratch_shapes=[w, w, m, m],
        compiler_params=pltpu.CompilerParams(vmem_limit_bytes=32 << 20),
        name="tile_turns",
    )(plan, users, items, days, counts)


def scatter_kernel(
    phi_ref, user_ref, total_ref, out_ref,
    other, out_near, near, kept, out_far, far, deep,
    o_s, o_r, n_s, n_r, f_s, f_r, d_s, d_r,
):
    me = place()
    x, y, z, c = me
    p, q = pick(c, y, x), pick(c, x, y)
    greet(me)
    welcome()
    sibling = device(x, y, z, 1 - c)
    crossed, nears, fars = {}, {}, {}

    def cross(kq):
        for kp in STEPS:
            pp, qq = lax.rem(q + kp, NX), lax.rem(p + kq, NX)
            src = phi_ref.at[pick(c, pp, qq), :, pick(c, qq, pp), 1 - c]
            crossed[kp, kq] = send(src, other.at[kp, kq], (o_s, o_r), (kp, kq), sibling)

    cross(STEPS[0])
    for turn, kq in enumerate(STEPS):
        if turn + 1 < NX:
            cross(STEPS[turn + 1])
        for kp in STEPS:
            pp, qq = lax.rem(p + kp, NX), lax.rem(q + kq, NX)
            crossed[kp, kq].wait_recv()
            piece = phi_ref[pick(c, qq, pp), :, pick(c, pp, qq), c] + other[kp, kq]
            if kp:
                out_near[kp - 1, kq] = piece.reshape(NZ * ROWS, R).astype(jnp.bfloat16)
                nears[kp, kq] = send(
                    out_near.at[kp - 1, kq], near.at[kp - 1, kq], (n_s, n_r), (kp - 1, kq),
                    along(1 - c, me, kp),
                )
            else:
                kept[kq] = piece
    for kq in STEPS:
        piece = kept[kq]
        for kp in (1, 3, 2):
            nears[kp, kq].wait_recv()
            piece += near[kp - 1, kq].astype(jnp.float32).reshape(NZ, ROWS, R)
        if kq:
            out_far[kq - 1] = piece.reshape(NZ * ROWS, R).astype(jnp.bfloat16)
            fars[kq] = send(out_far.at[kq - 1], far.at[kq - 1], (f_s, f_r), kq - 1, along(c, me, kq))
        else:
            kept[0] = piece
    for kq in (1, 2, 3):
        fars[kq].wait_recv()
    arrived = jnp.sum(far[...].astype(jnp.float32), axis=0)
    kept[0] += arrived.reshape(NZ, ROWS, R)
    deeps = []
    for step in range(1, NZ):
        there = lax.rem(z + step, NZ)
        deeps.append(
            send(kept.at[0, there], deep.at[step - 1], (d_s, d_r), step - 1,
                 device(x, y, there, c))
        )
    totals = total_ref[0:4, :] * total_ref[4:8, :] * (1.0 / (NX * NZ * NY * NC))
    for copy in deeps:
        copy.wait_recv()
    summed = kept[0, z] + jnp.sum(deep[...], axis=0)
    for part in range(R // 128):
        lanes = slice(part * 128, (part + 1) * 128)
        out_ref[:, lanes] = user_ref[:, lanes] * summed[:, lanes] / totals[part : part + 1, :]
    for group in (crossed.values(), nears.values(), fars.values(), deeps):
        for copy in group:
            copy.wait_send()


def scatter_call(phi, user_factors, totals):
    dma = pltpu.SemaphoreType.DMA
    vmem = pl.BlockSpec(memory_space=pltpu.VMEM)
    piece = (NZ, ROWS, R)
    return pl.pallas_call(
        scatter_kernel,
        out_shape=jax.ShapeDtypeStruct((ROWS, R), jnp.float32),
        in_specs=[vmem] * 3,
        out_specs=vmem,
        scratch_shapes=[
            pltpu.VMEM((NX, NX) + piece, jnp.float32),
            pltpu.VMEM((NX - 1, NX, NZ * ROWS, R), jnp.bfloat16),
            pltpu.VMEM((NX - 1, NX, NZ * ROWS, R), jnp.bfloat16),
            pltpu.VMEM((NX,) + piece, jnp.float32),
            pltpu.VMEM((NX - 1, NZ * ROWS, R), jnp.bfloat16),
            pltpu.VMEM((NX - 1, NZ * ROWS, R), jnp.bfloat16),
            pltpu.VMEM((NZ - 1, ROWS, R), jnp.float32),
            dma((NX, NX)), dma((NX, NX)),
            dma((NX - 1, NX)), dma((NX - 1, NX)),
            dma((NX - 1,)), dma((NX - 1,)),
            dma((NZ - 1,)), dma((NZ - 1,)),
        ],
        compiler_params=pltpu.CompilerParams(
            collective_id=1, has_side_effects=True, vmem_limit_bytes=24 << 20
        ),
        name="sum_phi",
    )(phi, user_factors, totals)


def per_device(user_factors, item_factors, day_factors, tile_counts, tile_index, tile_live):
    in_hbm = functools.partial(pltpu.with_memory_space_constraint, memory_space=pltpu.HBM)
    users, items, days, counts, plan, totals = gather_call(
        *map(in_hbm, (user_factors, item_factors, day_factors, tile_counts, tile_index)), tile_live
    )
    phi = phi_call(
        plan, users.reshape(NX * NZ, TILE // 2, R), items.reshape(ITEMBLK_DEV, TILE, R), days, counts
    )
    return scatter_call(phi.reshape(NX, NZ, NY, NC, ROWS, R), user_factors, totals)


def solution(mesh):
    in_specs = (
        P(("item", "day"), None),
        P("item", None),
        P("day", None),
        P(("item", "day"), None, None),
        P(None, ("item", "day")),
        P(("item", "day")),
    )
    out_specs = P(("item", "day"), None)
    return jax.shard_map(
        per_device, mesh=mesh, in_specs=in_specs, out_specs=out_specs, check_vma=False
    )
```

```python
import functools

import jax
import jax.numpy as jnp
from jax import lax
from jax.experimental import pallas as pl
from jax.experimental.pallas import tpu as pltpu
from jax.sharding import PartitionSpec as P

MESH = pl.DeviceIdType.MESH
R = 512
TILE = 128
CAP = 128
USER_BLOCKS = 16
DAY_DEV = 46
ITEMBLK_DEV = 4
NX, NY, NZ, NC = 4, 4, 8, 2
ROWS = 8
FOUR = 4
KEEP = 64
DAY_ROWS = 48
STEPS = (2, 1, 3, 0)
SHARES = (pl.ds(0, 5), pl.ds(5, 3))


def place():
    item, day = lax.axis_index("item"), lax.axis_index("day")
    x, z = lax.div(item, NZ), lax.rem(item, NZ)
    y, c = lax.div(day, NC), lax.rem(day, NC)
    return x, y, z, c


def device(x, y, z, c):
    return (x * NZ + z, y * NC + c)


def pick(c, zero, one):
    return zero + c * (one - zero)


def along(first, me, step):
    x, y, z, c = me
    return device(
        pick(first, lax.rem(x + step, NX), x), pick(first, y, lax.rem(y + step, NY)), z, c
    )


def z_place(ahead):
    return (0, 1, 3, 5, 7, 6, 4, 2)[ahead]


def greet(me):
    x, y, z, c = me
    barrier = pltpu.get_barrier_semaphore()
    for step in range(1, NZ):
        pl.semaphore_signal(
            barrier, inc=1, device_id=device(x, y, lax.rem(z + step, NZ), c), device_id_type=MESH
        )
    for step in range(1, NX):
        for first in (0, 1):
            pl.semaphore_signal(
                barrier, inc=1, device_id=along(first, me, step), device_id_type=MESH
            )
    pl.semaphore_signal(barrier, inc=1, device_id=device(x, y, z, 1 - c), device_id_type=MESH)


def welcome():
    pl.semaphore_wait(pltpu.get_barrier_semaphore(), NZ - 1 + 2 * (NX - 1) + 1)


def send(src, dst, sems, spot, target):
    copy = pltpu.make_async_remote_copy(
        src_ref=src,
        dst_ref=dst,
        send_sem=sems[0].at[spot],
        recv_sem=sems[1].at[spot],
        device_id=target,
        device_id_type=MESH,
    )
    copy.start()
    return copy


def order_slots(mine, theirs):
    lane = lax.broadcasted_iota(jnp.int32, (1, CAP), 1)

    def kept(live, other):
        return jnp.minimum(live, jnp.maximum(KEEP, lax.shift_right_logical(live + other + 1, 1)))

    live, other = mine[3:4], theirs[3:4]
    own = lane < kept(live, other)
    taken = (lane >= kept(other, live)) & (lane < other)
    users = jnp.concatenate(
        [jnp.where(own, mine[0:1], USER_BLOCKS), jnp.where(taken, theirs[0:1], USER_BLOCKS)], axis=1
    )
    rest = jnp.concatenate(
        [
            1 + lane + 256 * mine[0:1] + 4096 * mine[1:2] + 16384 * mine[2:3],
            1 + lane + KEEP + 256 * theirs[0:1] + 4096 * theirs[1:2] + 16384 * (theirs[2:3] + DAY_ROWS),
        ],
        axis=1,
    )
    first = lax.broadcasted_iota(jnp.int32, (2 * CAP, 2 * CAP), 0)
    second = lax.broadcasted_iota(jnp.int32, (2 * CAP, 2 * CAP), 1)

    def column(row):
        return jnp.sum(jnp.where(first == second, row, 0), axis=1, keepdims=True)

    same = (column(users) == users) & (first < second)
    rank = jnp.sum(same.astype(jnp.int32), axis=0, keepdims=True)
    block = lax.broadcasted_iota(jnp.int32, (USER_BLOCKS, 2 * CAP), 0)
    sizes = jnp.sum((block == users).astype(jnp.int32), axis=1, keepdims=True)
    padded = lax.shift_left(lax.shift_right_logical(sizes + (FOUR - 1), 2), 2)
    before = jnp.sum(jnp.where(block < users, padded, 0), axis=0, keepdims=True)
    spot = column(jnp.where(users < USER_BLOCKS, before + rank, 2 * CAP))
    codes = jnp.sum(jnp.where(spot == second, column(rest), 0), axis=0, keepdims=True)
    groups = jnp.sum(lax.shift_right_logical(padded, 2), axis=0, keepdims=True)
    return codes[:, :CAP], codes[:, CAP:], jnp.broadcast_to(groups, (1, CAP))


def user_places(z):
    lane = lax.broadcasted_iota(jnp.int32, (1, CAP), 1)
    ahead = ((lane & 7) - z) & (NZ - 1)
    spot = jnp.where(ahead <= NZ // 2, jnp.maximum(2 * ahead - 1, 0), 2 * (NZ - ahead))
    return (lane - (lane & 7)) + spot


def gather_kernel(
    user_hbm, item_hbm, day_hbm, counts_hbm, index_hbm, live_ref,
    users, items, days, counts, plan, total_ref,
    user_ref, day_ref, index_ref, meta, meta_in, sums, sums_c, sums_b, sums_a, sums_z,
    local_sem, z_s, z_r, a_s, a_r, b_s, b_r, c_s, c_r, m_s, m_r,
    tc_s, tc_r, tb_s, tb_r, ta_s, ta_r, tz_s, tz_r,
):
    me = place()
    x, y, z, c = me
    load_user, load_index, load_day, load_items, load_counts = (
        pltpu.make_async_copy(src, dst, local_sem.at[spot])
        for spot, (src, dst) in enumerate((
            (user_hbm, user_ref), (index_hbm, index_ref), (day_hbm, day_ref),
            (item_hbm, items), (counts_hbm, counts.at[pl.ds(0, CAP)]),
        ))
    )
    for copy in (load_user, load_index, load_day, load_items, load_counts):
        copy.start()
    greet(me)
    load_user.wait()
    users[x, 0, y, c] = user_ref[...].astype(jnp.bfloat16)
    welcome()
    other = device(x, y, z, 1 - c)

    a, b = pick(c, x, y), pick(c, y, x)

    def piece(back_a, back_b, share):
        a_from, b_from = lax.rem(a - back_a + NX, NX), lax.rem(b - back_b + NX, NX)
        return users.at[pick(c, a_from, b_from), SHARES[share], pick(c, b_from, a_from), c]

    def forward(back_a, share):
        spot = piece(back_a, 0, share)
        for step in (2, 1, 3):
            along_b[step, back_a, share] = send(
                spot, spot, (b_s, b_r), (step - 1, back_a, share), along(1 - c, me, step)
            )
        cross(back_a, 0, share)

    def cross(back_a, back_b, share):
        spot = piece(back_a, back_b, share)
        passed.append(send(spot, spot, (c_s, c_r), (back_a, back_b, share), other))

    def spread(share):
        spot = piece(0, 0, share)
        for step in (2, 1, 3):
            along_a[step, share] = send(
                spot, spot, (a_s, a_r), (step - 1, share), along(c, me, step)
            )
        forward(0, share)

    along_a, along_b, passed = {}, {}, []
    along_z = {
        step: send(
            users.at[x, 0, y, c], users.at[x, z_place(NZ - step), y, c], (z_s, z_r), step - 1,
            device(x, y, lax.rem(z + step, NZ), c),
        )
        for step in (2, 6, 1, 7, 4, 3, 5)
    }
    load_index.wait()
    load_day.wait()
    days[0:DAY_DEV, :] = day_ref[...].astype(jnp.float32)
    days[DAY_DEV:DAY_ROWS, :] = jnp.zeros((DAY_ROWS - DAY_DEV, R), jnp.float32)
    meta[...] = jnp.zeros_like(meta)
    meta[0:3, :] = index_ref[...]
    meta[3:4, :] = jnp.full((1, CAP), live_ref[0], jnp.int32)
    swapped = [
        send(meta, meta_in, (m_s, m_r), 0, other),
        send(days.at[pl.ds(0, DAY_ROWS)], days.at[pl.ds(DAY_ROWS, DAY_ROWS)], (m_s, m_r), 1, other),
        send(
            counts_hbm.at[pl.ds(KEEP, CAP - KEEP)], counts.at[pl.ds(CAP, CAP - KEEP)],
            (m_s, m_r), 2, other,
        ),
    ]
    load_items.wait()
    item_sum = jnp.sum(items[...].astype(jnp.float32), axis=0, keepdims=True)
    day_sum = jnp.sum(day_ref[...].astype(jnp.float32), axis=0, keepdims=True)
    for part in range(R // 128):
        lanes = slice(part * 128, (part + 1) * 128)
        sums[part : part + 1, :] = item_sum[:, lanes]
        sums[part + 4 : part + 5, :] = day_sum[:, lanes]
    add = send(sums, sums_c, (tc_s, tc_r), 0, other)

    for step in (7, 1, 6, 2):
        along_z[step].wait()
    spread(0)
    add.wait()
    sums[...] += sums_c[...]
    adds = [
        send(sums, sums_b.at[step - 1], (tb_s, tb_r), step - 1, along(1 - c, me, step))
        for step in range(1, NX)
    ]
    for step in (5, 3, 4):
        along_z[step].wait()
    spread(1)
    for copy in adds:
        copy.wait()
    sums[...] += jnp.sum(sums_b[...], axis=0)
    adds = [
        send(sums, sums_a.at[step - 1], (ta_s, ta_r), step - 1, along(c, me, step))
        for step in range(1, NX)
    ]
    for share in (0, 1):
        for step in (1, 3, 2):
            along_a[step, share].wait()
            forward(step, share)
    for copy in adds:
        copy.wait()
    sums[...] += jnp.sum(sums_a[...], axis=0)
    adds = [
        send(sums, sums_z.at[step - 1], (tz_s, tz_r), step - 1, device(x, y, lax.rem(z + step, NZ), c))
        for step in range(1, NZ)
    ]
    swapped[0].wait()
    first, second, groups = order_slots(meta[...], meta_in[...])
    plan[0:1, :] = first
    plan[1:2, :] = second
    plan[2:3, :] = groups
    plan[3:4, :] = user_places(z)
    plan[4:8, :] = jnp.zeros((4, CAP), jnp.int32)

    for back_a, share in ((0, 0), (0, 1), (1, 0), (3, 0), (2, 0), (1, 1), (3, 1), (2, 1)):
        for step in (1, 3, 2):
            along_b[step, back_a, share].wait()
            cross(back_a, step, share)
    for copy in adds:
        copy.wait()
    total_ref[...] = sums[...] + jnp.sum(sums_z[...], axis=0)
    swapped[1].wait()
    swapped[2].wait()
    load_counts.wait()
    for copy in passed:
        copy.wait()


def gather_call(user_factors, item_factors, day_factors, tile_counts, tile_index, tile_live):
    dma = pltpu.SemaphoreType.DMA
    vmem = pl.BlockSpec(memory_space=pltpu.VMEM)
    hbm = pl.BlockSpec(memory_space=pltpu.HBM)
    tile = (8, 128)
    return pl.pallas_call(
        gather_kernel,
        out_shape=(
            pltpu.VMEM((NX, NZ, NY, NC, ROWS, R), jnp.bfloat16),
            pltpu.VMEM((ITEMBLK_DEV * TILE, R), jnp.bfloat16),
            pltpu.VMEM((2 * DAY_ROWS, R), jnp.float32),
            pltpu.VMEM((2 * CAP - KEEP, TILE, TILE), jnp.bfloat16),
            pltpu.VMEM(tile, jnp.int32),
            pltpu.VMEM(tile, jnp.float32),
        ),
        in_specs=[hbm] * 5 + [pl.BlockSpec(memory_space=pltpu.SMEM)],
        out_specs=(vmem,) * 6,
        scratch_shapes=[
            pltpu.VMEM((ROWS, R), jnp.float32),
            pltpu.VMEM((DAY_DEV, R), jnp.bfloat16),
            pltpu.VMEM((3, CAP), jnp.int32),
            pltpu.VMEM(tile, jnp.int32),
            pltpu.VMEM(tile, jnp.int32),
            pltpu.VMEM(tile, jnp.float32),
            pltpu.VMEM(tile, jnp.float32),
            pltpu.VMEM((NX - 1,) + tile, jnp.float32),
            pltpu.VMEM((NX - 1,) + tile, jnp.float32),
            pltpu.VMEM((NZ - 1,) + tile, jnp.float32),
            dma((5,)),
        ]
        + [dma((NZ - 1,))] * 2 + [dma((NX - 1, 2))] * 2 + [dma((NX - 1, NX, 2))] * 2
        + [dma((NX, NX, 2))] * 2 + [dma((3,))] * 2
        + [dma((1,))] * 2 + [dma((NX - 1,))] * 4 + [dma((NZ - 1,))] * 2,
        compiler_params=pltpu.CompilerParams(
            collective_id=0, has_side_effects=True, vmem_limit_bytes=8 << 20
        ),
        name="gather_users",
    )(user_factors, item_factors, day_factors, tile_counts, tile_index, tile_live)


def phi_kernel(
    plan_ref, users_ref, item_ref, day_ref, counts_ref, phi_ref, w_even, w_odd, m_even, m_odd
):
    phi_ref[...] = jnp.zeros_like(phi_ref)
    groups = plan_ref[2, 0]

    def user_rows(block):
        return jnp.concatenate([users_ref[plan_ref[3, 2 * block + half]] for half in (0, 1)], axis=0)

    def codes(group):
        spot = FOUR * group
        row, col = lax.shift_right_logical(spot, 7), spot & (CAP - 1)
        return [plan_ref[row, col + part] for part in range(FOUR)]

    def user_block(code):
        return lax.shift_right_logical(jnp.maximum(code - 1, 0), 8) & (USER_BLOCKS - 1)

    def forward(group, w, m):
        group_codes = codes(group)
        for part, code in enumerate(group_codes):
            code = jnp.maximum(code - 1, 0)
            items = item_ref[lax.shift_right_logical(code, 12) & 3]
            scale = day_ref[pl.ds(lax.shift_right_logical(code, 14), 1), :]
            scale = jnp.broadcast_to(scale, (16, R)).astype(jnp.bfloat16)
            scaled = items.reshape(TILE // 16, 16, R) * scale[None]
            w[part * TILE : (part + 1) * TILE, :] = scaled.reshape(TILE, R)
        m[...] = lax.dot_general(
            user_rows(user_block(group_codes[0])), w[...], (((1,), (1,)), ((), ())),
            preferred_element_type=jnp.float32,
        )

    def backward(group, w, m):
        group_codes = codes(group)
        ratios = []
        for part, code in enumerate(group_codes):
            tile = counts_ref[jnp.maximum(code - 1, 0) & 255].astype(jnp.float32)
            ratio = tile / m[:, part * TILE : (part + 1) * TILE]
            ratios.append(jnp.where(code > 0, ratio, 0.0).astype(jnp.bfloat16))
        phi_ref[user_block(group_codes[0])] += jnp.dot(
            jnp.concatenate(ratios, axis=1), w[...], preferred_element_type=jnp.float32
        )

    forward(0, w_even, m_even)

    def turn(pair, carry):
        group = 2 * pair
        forward(group + 1, w_odd, m_odd)
        backward(group, w_even, m_even)
        forward(group + 2, w_even, m_even)
        backward(group + 1, w_odd, m_odd)
        return carry

    lax.fori_loop(0, lax.shift_right_logical(groups + 1, 1), turn, 0)


def phi_call(plan, users, items, days, counts):
    vmem = pl.BlockSpec(memory_space=pltpu.VMEM)
    w = pltpu.VMEM((FOUR * TILE, R), jnp.bfloat16)
    m = pltpu.VMEM((TILE, FOUR * TILE), jnp.float32)
    return pl.pallas_call(
        phi_kernel,
        out_shape=pltpu.VMEM((USER_BLOCKS, TILE, R), jnp.float32),
        in_specs=[pl.BlockSpec(memory_space=pltpu.SMEM)] + [vmem] * 4,
        out_specs=vmem,
        scratch_shapes=[w, w, m, m],
        compiler_params=pltpu.CompilerParams(vmem_limit_bytes=32 << 20),
        name="tile_turns",
    )(plan, users, items, days, counts)


def scatter_kernel(
    phi_ref, user_ref, total_ref, out_ref,
    other, out_near, near, kept, out_far, far, deep,
    o_s, o_r, n_s, n_r, f_s, f_r, d_s, d_r,
):
    me = place()
    x, y, z, c = me
    p, q = pick(c, y, x), pick(c, x, y)
    greet(me)
    welcome()
    sibling = device(x, y, z, 1 - c)
    crossed, nears, fars = {}, {}, {}

    def cross(kq):
        for kp in STEPS:
            pp, qq = lax.rem(q + kp, NX), lax.rem(p + kq, NX)
            src = phi_ref.at[pick(c, pp, qq), :, pick(c, qq, pp), 1 - c]
            crossed[kp, kq] = send(src, other.at[kp, kq], (o_s, o_r), (kp, kq), sibling)

    cross(STEPS[0])
    for turn, kq in enumerate(STEPS):
        if turn + 1 < NX:
            cross(STEPS[turn + 1])
        for kp in STEPS:
            pp, qq = lax.rem(p + kp, NX), lax.rem(q + kq, NX)
            crossed[kp, kq].wait_recv()
            piece = phi_ref[pick(c, qq, pp), :, pick(c, pp, qq), c] + other[kp, kq]
            if kp:
                out_near[kp - 1, kq] = piece.reshape(NZ * ROWS, R).astype(jnp.bfloat16)
                nears[kp, kq] = send(
                    out_near.at[kp - 1, kq], near.at[kp - 1, kq], (n_s, n_r), (kp - 1, kq),
                    along(1 - c, me, kp),
                )
            else:
                kept[kq] = piece
    for kq in STEPS:
        piece = kept[kq]
        for kp in (1, 3, 2):
            nears[kp, kq].wait_recv()
            piece += near[kp - 1, kq].astype(jnp.float32).reshape(NZ, ROWS, R)
        if kq:
            out_far[kq - 1] = piece.reshape(NZ * ROWS, R).astype(jnp.bfloat16)
            fars[kq] = send(out_far.at[kq - 1], far.at[kq - 1], (f_s, f_r), kq - 1, along(c, me, kq))
        else:
            kept[0] = piece
    for kq in (1, 2, 3):
        fars[kq].wait_recv()
    arrived = jnp.sum(far[...].astype(jnp.float32), axis=0)
    kept[0] += arrived.reshape(NZ, ROWS, R)
    deeps = []
    for step in range(1, NZ):
        there = lax.rem(z + step, NZ)
        deeps.append(
            send(kept.at[0, there], deep.at[step - 1], (d_s, d_r), step - 1,
                 device(x, y, there, c))
        )
    totals = total_ref[0:4, :] * total_ref[4:8, :] * (1.0 / (NX * NZ * NY * NC))
    for copy in deeps:
        copy.wait_recv()
    summed = kept[0, z] + jnp.sum(deep[...], axis=0)
    for part in range(R // 128):
        lanes = slice(part * 128, (part + 1) * 128)
        out_ref[:, lanes] = user_ref[:, lanes] * summed[:, lanes] / totals[part : part + 1, :]
    for group in (crossed.values(), nears.values(), fars.values(), deeps):
        for copy in group:
            copy.wait_send()


def scatter_call(phi, user_factors, totals):
    dma = pltpu.SemaphoreType.DMA
    vmem = pl.BlockSpec(memory_space=pltpu.VMEM)
    piece = (NZ, ROWS, R)
    return pl.pallas_call(
        scatter_kernel,
        out_shape=jax.ShapeDtypeStruct((ROWS, R), jnp.float32),
        in_specs=[vmem] * 3,
        out_specs=vmem,
        scratch_shapes=[
            pltpu.VMEM((NX, NX) + piece, jnp.float32),
            pltpu.VMEM((NX - 1, NX, NZ * ROWS, R), jnp.bfloat16),
            pltpu.VMEM((NX - 1, NX, NZ * ROWS, R), jnp.bfloat16),
            pltpu.VMEM((NX,) + piece, jnp.float32),
            pltpu.VMEM((NX - 1, NZ * ROWS, R), jnp.bfloat16),
            pltpu.VMEM((NX - 1, NZ * ROWS, R), jnp.bfloat16),
            pltpu.VMEM((NZ - 1, ROWS, R), jnp.float32),
            dma((NX, NX)), dma((NX, NX)),
            dma((NX - 1, NX)), dma((NX - 1, NX)),
            dma((NX - 1,)), dma((NX - 1,)),
            dma((NZ - 1,)), dma((NZ - 1,)),
        ],
        compiler_params=pltpu.CompilerParams(
            collective_id=1, has_side_effects=True, vmem_limit_bytes=24 << 20
        ),
        name="sum_phi",
    )(phi, user_factors, totals)


def per_device(user_factors, item_factors, day_factors, tile_counts, tile_index, tile_live):
    in_hbm = functools.partial(pltpu.with_memory_space_constraint, memory_space=pltpu.HBM)
    users, items, days, counts, plan, totals = gather_call(
        *map(in_hbm, (user_factors, item_factors, day_factors, tile_counts, tile_index)), tile_live
    )
    phi = phi_call(
        plan, users.reshape(NX * NZ, TILE // 2, R), items.reshape(ITEMBLK_DEV, TILE, R), days, counts
    )
    return scatter_call(phi.reshape(NX, NZ, NY, NC, ROWS, R), user_factors, totals)


def solution(mesh):
    in_specs = (
        P(("item", "day"), None),
        P("item", None),
        P("day", None),
        P(("item", "day"), None, None),
        P(None, ("item", "day")),
        P(("item", "day")),
    )
    out_specs = P(("item", "day"), None)
    return jax.shard_map(
        per_device, mesh=mesh, in_specs=in_specs, out_specs=out_specs, check_vma=False
    )
```

```python
import functools

import jax
import jax.numpy as jnp
from jax import lax
from jax.experimental import pallas as pl
from jax.experimental.pallas import tpu as pltpu
from jax.sharding import PartitionSpec as P

MESH = pl.DeviceIdType.MESH
R = 512
TILE = 128
CAP = 128
USER_BLOCKS = 16
DAY_DEV = 46
ITEMBLK_DEV = 4
NX, NY, NZ, NC = 4, 4, 8, 2
ROWS = 8
FOUR = 4
KEEP = 64
DAY_ROWS = 48
STEPS = (2, 1, 3, 0)
SHARES = (pl.ds(0, 5), pl.ds(5, 3))


def place():
    item, day = lax.axis_index("item"), lax.axis_index("day")
    x, z = lax.div(item, NZ), lax.rem(item, NZ)
    y, c = lax.div(day, NC), lax.rem(day, NC)
    return x, y, z, c


def device(x, y, z, c):
    return (x * NZ + z, y * NC + c)


def pick(c, zero, one):
    return zero + c * (one - zero)


def along(first, me, step):
    x, y, z, c = me
    return device(
        pick(first, lax.rem(x + step, NX), x), pick(first, y, lax.rem(y + step, NY)), z, c
    )


def z_place(ahead):
    return (0, 1, 3, 5, 7, 6, 4, 2)[ahead]


def greet(me):
    x, y, z, c = me
    barrier = pltpu.get_barrier_semaphore()
    for step in (4, 3, 5, 2, 6, 1, 7):
        pl.semaphore_signal(
            barrier, inc=1, device_id=device(x, y, lax.rem(z + step, NZ), c), device_id_type=MESH
        )
    for step in range(1, NX):
        for first in (0, 1):
            pl.semaphore_signal(
                barrier, inc=1, device_id=along(first, me, step), device_id_type=MESH
            )
    pl.semaphore_signal(barrier, inc=1, device_id=device(x, y, z, 1 - c), device_id_type=MESH)


def welcome():
    pl.semaphore_wait(pltpu.get_barrier_semaphore(), NZ - 1 + 2 * (NX - 1) + 1)


def send(src, dst, sems, spot, target):
    copy = pltpu.make_async_remote_copy(
        src_ref=src,
        dst_ref=dst,
        send_sem=sems[0].at[spot],
        recv_sem=sems[1].at[spot],
        device_id=target,
        device_id_type=MESH,
    )
    copy.start()
    return copy


def order_slots(mine, theirs):
    lane = lax.broadcasted_iota(jnp.int32, (1, CAP), 1)

    def kept(live, other):
        return jnp.minimum(live, jnp.maximum(KEEP, lax.shift_right_logical(live + other + 1, 1)))

    live, other = mine[3:4], theirs[3:4]
    own = lane < kept(live, other)
    taken = (lane >= kept(other, live)) & (lane < other)
    users = jnp.concatenate(
        [jnp.where(own, mine[0:1], USER_BLOCKS), jnp.where(taken, theirs[0:1], USER_BLOCKS)], axis=1
    )
    rest = jnp.concatenate(
        [
            1 + lane + 256 * mine[0:1] + 4096 * mine[1:2] + 16384 * mine[2:3],
            1 + lane + KEEP + 256 * theirs[0:1] + 4096 * theirs[1:2] + 16384 * (theirs[2:3] + DAY_ROWS),
        ],
        axis=1,
    )
    first = lax.broadcasted_iota(jnp.int32, (2 * CAP, 2 * CAP), 0)
    second = lax.broadcasted_iota(jnp.int32, (2 * CAP, 2 * CAP), 1)

    def column(row):
        return jnp.sum(jnp.where(first == second, row, 0), axis=1, keepdims=True)

    same = (column(users) == users) & (first < second)
    rank = jnp.sum(same.astype(jnp.int32), axis=0, keepdims=True)
    block = lax.broadcasted_iota(jnp.int32, (USER_BLOCKS, 2 * CAP), 0)
    sizes = jnp.sum((block == users).astype(jnp.int32), axis=1, keepdims=True)
    padded = lax.shift_left(lax.shift_right_logical(sizes + (FOUR - 1), 2), 2)
    before = jnp.sum(jnp.where(block < users, padded, 0), axis=0, keepdims=True)
    spot = column(jnp.where(users < USER_BLOCKS, before + rank, 2 * CAP))
    codes = jnp.sum(jnp.where(spot == second, column(rest), 0), axis=0, keepdims=True)
    groups = jnp.sum(lax.shift_right_logical(padded, 2), axis=0, keepdims=True)
    return codes[:, :CAP], codes[:, CAP:], jnp.broadcast_to(groups, (1, CAP))


def user_places(z):
    lane = lax.broadcasted_iota(jnp.int32, (1, CAP), 1)
    ahead = ((lane & 7) - z) & (NZ - 1)
    spot = jnp.where(ahead <= NZ // 2, jnp.maximum(2 * ahead - 1, 0), 2 * (NZ - ahead))
    return (lane - (lane & 7)) + spot


def gather_kernel(
    user_hbm, item_hbm, day_hbm, counts_hbm, index_hbm, live_ref,
    users, items, days, counts, plan_smem, total_ref,
    user_ref, day_ref, index_ref, plan, meta, meta_in, sums, sums_c, sums_b, sums_a, sums_z,
    local_sem, z_s, z_r, a_s, a_r, b_s, b_r, c_s, c_r, m_s, m_r,
    tc_s, tc_r, tb_s, tb_r, ta_s, ta_r, tz_s, tz_r,
):
    me = place()
    x, y, z, c = me
    load_user, load_index, load_day, load_items, load_counts = (
        pltpu.make_async_copy(src, dst, local_sem.at[spot])
        for spot, (src, dst) in enumerate((
            (user_hbm, user_ref), (index_hbm, index_ref), (day_hbm, day_ref),
            (item_hbm, items), (counts_hbm, counts.at[pl.ds(0, CAP)]),
        ))
    )
    for copy in (load_user, load_index, load_day, load_items, load_counts):
        copy.start()
    greet(me)
    load_user.wait()
    users[x, 0, y, c] = user_ref[...].astype(jnp.bfloat16)
    welcome()
    other = device(x, y, z, 1 - c)

    a, b = pick(c, x, y), pick(c, y, x)

    def piece(back_a, back_b, share):
        a_from, b_from = lax.rem(a - back_a + NX, NX), lax.rem(b - back_b + NX, NX)
        return users.at[pick(c, a_from, b_from), SHARES[share], pick(c, b_from, a_from), c]

    def forward(back_a, share):
        spot = piece(back_a, 0, share)
        for step in (2, 1, 3):
            along_b[step, back_a, share] = send(
                spot, spot, (b_s, b_r), (step - 1, back_a, share), along(1 - c, me, step)
            )
        cross(back_a, 0, share)

    def cross(back_a, back_b, share):
        spot = piece(back_a, back_b, share)
        passed.append(send(spot, spot, (c_s, c_r), (back_a, back_b, share), other))

    def spread(share):
        spot = piece(0, 0, share)
        for step in (2, 1, 3):
            along_a[step, share] = send(
                spot, spot, (a_s, a_r), (step - 1, share), along(c, me, step)
            )
        forward(0, share)

    along_a, along_b, passed = {}, {}, []
    along_z = {
        step: send(
            users.at[x, 0, y, c], users.at[x, z_place(NZ - step), y, c], (z_s, z_r), step - 1,
            device(x, y, lax.rem(z + step, NZ), c),
        )
        for step in (2, 6, 1, 7, 4, 3, 5)
    }
    load_index.wait()
    load_day.wait()
    days[0:DAY_DEV, :] = day_ref[...].astype(jnp.float32)
    days[DAY_DEV:DAY_ROWS, :] = jnp.zeros((DAY_ROWS - DAY_DEV, R), jnp.float32)
    meta[...] = jnp.zeros_like(meta)
    meta[0:3, :] = index_ref[...]
    meta[3:4, :] = jnp.full((1, CAP), live_ref[0], jnp.int32)
    swapped = [
        send(meta, meta_in, (m_s, m_r), 0, other),
        send(days.at[pl.ds(0, DAY_ROWS)], days.at[pl.ds(DAY_ROWS, DAY_ROWS)], (m_s, m_r), 1, other),
        send(
            counts_hbm.at[pl.ds(KEEP, CAP - KEEP)], counts.at[pl.ds(CAP, CAP - KEEP)],
            (m_s, m_r), 2, other,
        ),
    ]
    load_items.wait()
    item_sum = jnp.sum(items[...].astype(jnp.float32), axis=0, keepdims=True)
    day_sum = jnp.sum(day_ref[...].astype(jnp.float32), axis=0, keepdims=True)
    for part in range(R // 128):
        lanes = slice(part * 128, (part + 1) * 128)
        sums[part : part + 1, :] = item_sum[:, lanes]
        sums[part + 4 : part + 5, :] = day_sum[:, lanes]
    add = send(sums, sums_c, (tc_s, tc_r), 0, other)

    for step in (7, 1, 6, 2):
        along_z[step].wait()
    spread(0)
    add.wait()
    sums[...] += sums_c[...]
    adds = [
        send(sums, sums_b.at[step - 1], (tb_s, tb_r), step - 1, along(1 - c, me, step))
        for step in range(1, NX)
    ]
    for step in (5, 3, 4):
        along_z[step].wait()
    spread(1)
    for copy in adds:
        copy.wait()
    sums[...] += jnp.sum(sums_b[...], axis=0)
    adds = [
        send(sums, sums_a.at[step - 1], (ta_s, ta_r), step - 1, along(c, me, step))
        for step in range(1, NX)
    ]
    for share in (0, 1):
        for step in (1, 3, 2):
            along_a[step, share].wait()
            forward(step, share)
    for copy in adds:
        copy.wait()
    sums[...] += jnp.sum(sums_a[...], axis=0)
    adds = [
        send(sums, sums_z.at[step - 1], (tz_s, tz_r), step - 1, device(x, y, lax.rem(z + step, NZ), c))
        for step in (4, 3, 5, 2, 6, 1, 7)
    ]
    swapped[0].wait()
    first, second, groups = order_slots(meta[...], meta_in[...])
    plan[0:1, :] = first
    plan[1:2, :] = second
    plan[2:3, :] = groups
    plan[3:4, :] = user_places(z)
    plan[4:8, :] = jnp.zeros((4, CAP), jnp.int32)
    hand_plan = pltpu.make_async_copy(plan, plan_smem, local_sem.at[5])
    hand_plan.start()

    for back_a, share in ((0, 0), (0, 1), (1, 0), (3, 0), (2, 0), (1, 1), (3, 1), (2, 1)):
        for step in (1, 3, 2):
            along_b[step, back_a, share].wait()
            cross(back_a, step, share)
    for copy in adds:
        copy.wait()
    total_ref[...] = sums[...] + jnp.sum(sums_z[...], axis=0)
    swapped[1].wait()
    swapped[2].wait()
    load_counts.wait()
    hand_plan.wait()
    for copy in passed:
        copy.wait()


def gather_call(user_factors, item_factors, day_factors, tile_counts, tile_index, tile_live):
    dma = pltpu.SemaphoreType.DMA
    vmem = pl.BlockSpec(memory_space=pltpu.VMEM)
    hbm = pl.BlockSpec(memory_space=pltpu.HBM)
    tile = (8, 128)
    return pl.pallas_call(
        gather_kernel,
        out_shape=(
            pltpu.VMEM((NX, NZ, NY, NC, ROWS, R), jnp.bfloat16),
            pltpu.VMEM((ITEMBLK_DEV * TILE, R), jnp.bfloat16),
            pltpu.VMEM((2 * DAY_ROWS, R), jnp.float32),
            pltpu.VMEM((2 * CAP - KEEP, TILE, TILE), jnp.bfloat16),
            pltpu.SMEM(tile, jnp.int32),
            pltpu.VMEM(tile, jnp.float32),
        ),
        in_specs=[hbm] * 5 + [pl.BlockSpec(memory_space=pltpu.SMEM)],
        out_specs=(vmem,) * 4 + (pl.BlockSpec(memory_space=pltpu.SMEM), vmem),
        scratch_shapes=[
            pltpu.VMEM((ROWS, R), jnp.float32),
            pltpu.VMEM((DAY_DEV, R), jnp.bfloat16),
            pltpu.VMEM((3, CAP), jnp.int32),
            pltpu.VMEM(tile, jnp.int32),
            pltpu.VMEM(tile, jnp.int32),
            pltpu.VMEM(tile, jnp.int32),
            pltpu.VMEM(tile, jnp.float32),
            pltpu.VMEM(tile, jnp.float32),
            pltpu.VMEM((NX - 1,) + tile, jnp.float32),
            pltpu.VMEM((NX - 1,) + tile, jnp.float32),
            pltpu.VMEM((NZ - 1,) + tile, jnp.float32),
            dma((6,)),
        ]
        + [dma((NZ - 1,))] * 2 + [dma((NX - 1, 2))] * 2 + [dma((NX - 1, NX, 2))] * 2
        + [dma((NX, NX, 2))] * 2 + [dma((3,))] * 2
        + [dma((1,))] * 2 + [dma((NX - 1,))] * 4 + [dma((NZ - 1,))] * 2,
        compiler_params=pltpu.CompilerParams(
            collective_id=0, has_side_effects=True, vmem_limit_bytes=8 << 20
        ),
        name="gather_users",
    )(user_factors, item_factors, day_factors, tile_counts, tile_index, tile_live)


def phi_kernel(
    plan_ref, users_ref, item_ref, day_ref, counts_ref, phi_ref, w_even, w_odd, m_even, m_odd
):
    phi_ref[...] = jnp.zeros_like(phi_ref)
    groups = plan_ref[2, 0]

    def user_rows(block):
        return jnp.concatenate([users_ref[plan_ref[3, 2 * block + half]] for half in (0, 1)], axis=0)

    def codes(group):
        spot = FOUR * group
        row, col = lax.shift_right_logical(spot, 7), spot & (CAP - 1)
        return [plan_ref[row, col + part] for part in range(FOUR)]

    def user_block(code):
        return lax.shift_right_logical(jnp.maximum(code - 1, 0), 8) & (USER_BLOCKS - 1)

    def forward(group, w, m):
        group_codes = codes(group)
        for part, code in enumerate(group_codes):
            code = jnp.maximum(code - 1, 0)
            items = item_ref[lax.shift_right_logical(code, 12) & 3]
            scale = day_ref[pl.ds(lax.shift_right_logical(code, 14), 1), :]
            scale = jnp.broadcast_to(scale, (16, R)).astype(jnp.bfloat16)
            scaled = items.reshape(TILE // 16, 16, R) * scale[None]
            w[part * TILE : (part + 1) * TILE, :] = scaled.reshape(TILE, R)
        m[...] = lax.dot_general(
            user_rows(user_block(group_codes[0])), w[...], (((1,), (1,)), ((), ())),
            preferred_element_type=jnp.float32,
        )

    def backward(group, w, m):
        group_codes = codes(group)
        ratios = []
        for part, code in enumerate(group_codes):
            tile = counts_ref[jnp.maximum(code - 1, 0) & 255].astype(jnp.float32)
            ratio = tile / m[:, part * TILE : (part + 1) * TILE]
            ratios.append(jnp.where(code > 0, ratio, 0.0).astype(jnp.bfloat16))
        phi_ref[user_block(group_codes[0])] += jnp.dot(
            jnp.concatenate(ratios, axis=1), w[...], preferred_element_type=jnp.float32
        )

    forward(0, w_even, m_even)

    def turn(pair, carry):
        group = 2 * pair
        forward(group + 1, w_odd, m_odd)
        backward(group, w_even, m_even)
        forward(group + 2, w_even, m_even)
        backward(group + 1, w_odd, m_odd)
        return carry

    lax.fori_loop(0, lax.shift_right_logical(groups + 1, 1), turn, 0)


def phi_call(plan, users, items, days, counts):
    vmem = pl.BlockSpec(memory_space=pltpu.VMEM)
    w = pltpu.VMEM((FOUR * TILE, R), jnp.bfloat16)
    m = pltpu.VMEM((TILE, FOUR * TILE), jnp.float32)
    return pl.pallas_call(
        phi_kernel,
        out_shape=pltpu.VMEM((USER_BLOCKS, TILE, R), jnp.float32),
        in_specs=[pl.BlockSpec(memory_space=pltpu.SMEM)] + [vmem] * 4,
        out_specs=vmem,
        scratch_shapes=[w, w, m, m],
        compiler_params=pltpu.CompilerParams(vmem_limit_bytes=32 << 20),
        name="tile_turns",
    )(plan, users, items, days, counts)


def scatter_kernel(
    phi_ref, user_ref, total_ref, out_ref,
    other, out_near, near, kept, out_far, far, deep,
    o_s, o_r, n_s, n_r, f_s, f_r, d_s, d_r,
):
    me = place()
    x, y, z, c = me
    p, q = pick(c, y, x), pick(c, x, y)
    greet(me)
    welcome()
    sibling = device(x, y, z, 1 - c)
    crossed, nears, fars = {}, {}, {}

    def cross(kq):
        for kp in STEPS:
            pp, qq = lax.rem(q + kp, NX), lax.rem(p + kq, NX)
            src = phi_ref.at[pick(c, pp, qq), :, pick(c, qq, pp), 1 - c]
            crossed[kp, kq] = send(src, other.at[kp, kq], (o_s, o_r), (kp, kq), sibling)

    cross(STEPS[0])
    for turn, kq in enumerate(STEPS):
        if turn + 1 < NX:
            cross(STEPS[turn + 1])
        for kp in STEPS:
            pp, qq = lax.rem(p + kp, NX), lax.rem(q + kq, NX)
            crossed[kp, kq].wait_recv()
            piece = phi_ref[pick(c, qq, pp), :, pick(c, pp, qq), c] + other[kp, kq]
            if kp:
                out_near[kp - 1, kq] = piece.reshape(NZ * ROWS, R).astype(jnp.bfloat16)
                nears[kp, kq] = send(
                    out_near.at[kp - 1, kq], near.at[kp - 1, kq], (n_s, n_r), (kp - 1, kq),
                    along(1 - c, me, kp),
                )
            else:
                kept[kq] = piece
    for kq in STEPS:
        piece = kept[kq]
        for kp in (1, 3, 2):
            nears[kp, kq].wait_recv()
            piece += near[kp - 1, kq].astype(jnp.float32).reshape(NZ, ROWS, R)
        if kq:
            out_far[kq - 1] = piece.reshape(NZ * ROWS, R).astype(jnp.bfloat16)
            fars[kq] = send(out_far.at[kq - 1], far.at[kq - 1], (f_s, f_r), kq - 1, along(c, me, kq))
        else:
            kept[0] = piece
    for kq in (1, 2, 3):
        fars[kq].wait_recv()
    arrived = jnp.sum(far[...].astype(jnp.float32), axis=0)
    kept[0] += arrived.reshape(NZ, ROWS, R)
    deeps = []
    for step in (4, 3, 5, 2, 6, 1, 7):
        there = lax.rem(z + step, NZ)
        deeps.append(
            send(kept.at[0, there], deep.at[step - 1], (d_s, d_r), step - 1,
                 device(x, y, there, c))
        )
    totals = total_ref[0:4, :] * total_ref[4:8, :] * (1.0 / (NX * NZ * NY * NC))
    for copy in deeps:
        copy.wait_recv()
    summed = kept[0, z] + jnp.sum(deep[...], axis=0)
    for part in range(R // 128):
        lanes = slice(part * 128, (part + 1) * 128)
        out_ref[:, lanes] = user_ref[:, lanes] * summed[:, lanes] / totals[part : part + 1, :]
    for group in (crossed.values(), nears.values(), fars.values(), deeps):
        for copy in group:
            copy.wait_send()


def scatter_call(phi, user_factors, totals):
    dma = pltpu.SemaphoreType.DMA
    vmem = pl.BlockSpec(memory_space=pltpu.VMEM)
    piece = (NZ, ROWS, R)
    return pl.pallas_call(
        scatter_kernel,
        out_shape=jax.ShapeDtypeStruct((ROWS, R), jnp.float32),
        in_specs=[vmem] * 3,
        out_specs=vmem,
        scratch_shapes=[
            pltpu.VMEM((NX, NX) + piece, jnp.float32),
            pltpu.VMEM((NX - 1, NX, NZ * ROWS, R), jnp.bfloat16),
            pltpu.VMEM((NX - 1, NX, NZ * ROWS, R), jnp.bfloat16),
            pltpu.VMEM((NX,) + piece, jnp.float32),
            pltpu.VMEM((NX - 1, NZ * ROWS, R), jnp.bfloat16),
            pltpu.VMEM((NX - 1, NZ * ROWS, R), jnp.bfloat16),
            pltpu.VMEM((NZ - 1, ROWS, R), jnp.float32),
            dma((NX, NX)), dma((NX, NX)),
            dma((NX - 1, NX)), dma((NX - 1, NX)),
            dma((NX - 1,)), dma((NX - 1,)),
            dma((NZ - 1,)), dma((NZ - 1,)),
        ],
        compiler_params=pltpu.CompilerParams(
            collective_id=1, has_side_effects=True, vmem_limit_bytes=24 << 20
        ),
        name="sum_phi",
    )(phi, user_factors, totals)


def per_device(user_factors, item_factors, day_factors, tile_counts, tile_index, tile_live):
    in_hbm = functools.partial(pltpu.with_memory_space_constraint, memory_space=pltpu.HBM)
    users, items, days, counts, plan, totals = gather_call(
        *map(in_hbm, (user_factors, item_factors, day_factors, tile_counts, tile_index)), tile_live
    )
    phi = phi_call(
        plan, users.reshape(NX * NZ, TILE // 2, R), items.reshape(ITEMBLK_DEV, TILE, R), days, counts
    )
    return scatter_call(phi.reshape(NX, NZ, NY, NC, ROWS, R), user_factors, totals)


def solution(mesh):
    in_specs = (
        P(("item", "day"), None),
        P("item", None),
        P("day", None),
        P(("item", "day"), None, None),
        P(None, ("item", "day")),
        P(("item", "day")),
    )
    out_specs = P(("item", "day"), None)
    return jax.shard_map(
        per_device, mesh=mesh, in_specs=in_specs, out_specs=out_specs, check_vma=False
    )
```

```python
import functools

import jax
import jax.numpy as jnp
from jax import lax
from jax.experimental import pallas as pl
from jax.experimental.pallas import tpu as pltpu
from jax.sharding import PartitionSpec as P

MESH = pl.DeviceIdType.MESH
R = 512
TILE = 128
CAP = 128
USER_BLOCKS = 16
DAY_DEV = 46
ITEMBLK_DEV = 4
NX, NY, NZ, NC = 4, 4, 8, 2
ROWS = 8
FOUR = 4
KEEP = 64
DAY_ROWS = 48
STEPS = (2, 1, 3, 0)
SHARES = (pl.ds(0, 5), pl.ds(5, 3))


def place():
    item, day = lax.axis_index("item"), lax.axis_index("day")
    x, z = lax.div(item, NZ), lax.rem(item, NZ)
    y, c = lax.div(day, NC), lax.rem(day, NC)
    return x, y, z, c


def device(x, y, z, c):
    return (x * NZ + z, y * NC + c)


def pick(c, zero, one):
    return zero + c * (one - zero)


def along(first, me, step):
    x, y, z, c = me
    return device(
        pick(first, lax.rem(x + step, NX), x), pick(first, y, lax.rem(y + step, NY)), z, c
    )


def z_place(ahead):
    return (0, 1, 3, 5, 7, 6, 4, 2)[ahead]


def greet(me):
    x, y, z, c = me
    barrier = pltpu.get_barrier_semaphore()
    for step in (4, 3, 5, 2, 6, 1, 7):
        pl.semaphore_signal(
            barrier, inc=1, device_id=device(x, y, lax.rem(z + step, NZ), c), device_id_type=MESH
        )
    for step in range(1, NX):
        for first in (0, 1):
            pl.semaphore_signal(
                barrier, inc=1, device_id=along(first, me, step), device_id_type=MESH
            )
    pl.semaphore_signal(barrier, inc=1, device_id=device(x, y, z, 1 - c), device_id_type=MESH)


def welcome():
    pl.semaphore_wait(pltpu.get_barrier_semaphore(), NZ - 1 + 2 * (NX - 1) + 1)


def send(src, dst, sems, spot, target):
    copy = pltpu.make_async_remote_copy(
        src_ref=src,
        dst_ref=dst,
        send_sem=sems[0].at[spot],
        recv_sem=sems[1].at[spot],
        device_id=target,
        device_id_type=MESH,
    )
    copy.start()
    return copy


def order_slots(mine, theirs):
    lane = lax.broadcasted_iota(jnp.int32, (1, CAP), 1)

    def kept(live, other):
        return jnp.minimum(live, jnp.maximum(KEEP, lax.shift_right_logical(live + other + 1, 1)))

    live, other = mine[3:4], theirs[3:4]
    own = lane < kept(live, other)
    taken = (lane >= kept(other, live)) & (lane < other)
    users = jnp.concatenate(
        [jnp.where(own, mine[0:1], USER_BLOCKS), jnp.where(taken, theirs[0:1], USER_BLOCKS)], axis=1
    )
    rest = jnp.concatenate(
        [
            1 + lane + 256 * mine[0:1] + 4096 * mine[1:2] + 16384 * mine[2:3],
            1 + lane + KEEP + 256 * theirs[0:1] + 4096 * theirs[1:2] + 16384 * (theirs[2:3] + DAY_ROWS),
        ],
        axis=1,
    )
    first = lax.broadcasted_iota(jnp.int32, (2 * CAP, 2 * CAP), 0)
    second = lax.broadcasted_iota(jnp.int32, (2 * CAP, 2 * CAP), 1)

    def column(row):
        return jnp.sum(jnp.where(first == second, row, 0), axis=1, keepdims=True)

    same = (column(users) == users) & (first < second)
    rank = jnp.sum(same.astype(jnp.int32), axis=0, keepdims=True)
    block = lax.broadcasted_iota(jnp.int32, (USER_BLOCKS, 2 * CAP), 0)
    sizes = jnp.sum((block == users).astype(jnp.int32), axis=1, keepdims=True)
    padded = lax.shift_left(lax.shift_right_logical(sizes + (FOUR - 1), 2), 2)
    before = jnp.sum(jnp.where(block < users, padded, 0), axis=0, keepdims=True)
    spot = column(jnp.where(users < USER_BLOCKS, before + rank, 2 * CAP))
    codes = jnp.sum(jnp.where(spot == second, column(rest), 0), axis=0, keepdims=True)
    groups = jnp.sum(lax.shift_right_logical(padded, 2), axis=0, keepdims=True)
    return codes[:, :CAP], codes[:, CAP:], jnp.broadcast_to(groups, (1, CAP))


def user_places(z):
    lane = lax.broadcasted_iota(jnp.int32, (1, CAP), 1)
    ahead = ((lane & 7) - z) & (NZ - 1)
    spot = jnp.where(ahead <= NZ // 2, jnp.maximum(2 * ahead - 1, 0), 2 * (NZ - ahead))
    return (lane - (lane & 7)) + spot


def gather_kernel(
    user_hbm, item_hbm, day_hbm, counts_hbm, index_hbm, live_ref,
    users, items, days, counts, plan_smem, total_ref,
    user_ref, day_ref, index_ref, plan, meta, meta_in, sums, sums_c, sums_b, sums_a, sums_z,
    local_sem, z_s, z_r, a_s, a_r, b_s, b_r, c_s, c_r, m_s, m_r,
    tc_s, tc_r, tb_s, tb_r, ta_s, ta_r, tz_s, tz_r,
):
    me = place()
    x, y, z, c = me
    load_user, load_index, load_day, load_items, load_counts = (
        pltpu.make_async_copy(src, dst, local_sem.at[spot])
        for spot, (src, dst) in enumerate((
            (user_hbm, user_ref), (index_hbm, index_ref), (day_hbm, day_ref),
            (item_hbm, items), (counts_hbm, counts.at[pl.ds(0, CAP)]),
        ))
    )
    for copy in (load_user, load_index, load_day, load_items, load_counts):
        copy.start()
    greet(me)
    load_user.wait()
    users[x, 0, y, c] = user_ref[...].astype(jnp.bfloat16)
    welcome()
    other = device(x, y, z, 1 - c)

    a, b = pick(c, x, y), pick(c, y, x)

    def piece(back_a, back_b, share):
        a_from, b_from = lax.rem(a - back_a + NX, NX), lax.rem(b - back_b + NX, NX)
        return users.at[pick(c, a_from, b_from), SHARES[share], pick(c, b_from, a_from), c]

    def forward(back_a, share):
        spot = piece(back_a, 0, share)
        for step in (2, 1, 3):
            along_b[step, back_a, share] = send(
                spot, spot, (b_s, b_r), (step - 1, back_a, share), along(1 - c, me, step)
            )
        cross(back_a, 0, share)

    def cross(back_a, back_b, share):
        spot = piece(back_a, back_b, share)
        passed.append(send(spot, spot, (c_s, c_r), (back_a, back_b, share), other))

    def spread(share):
        spot = piece(0, 0, share)
        for step in (2, 1, 3):
            along_a[step, share] = send(
                spot, spot, (a_s, a_r), (step - 1, share), along(c, me, step)
            )
        forward(0, share)

    along_a, along_b, passed = {}, {}, []
    along_z = {
        step: send(
            users.at[x, 0, y, c], users.at[x, z_place(NZ - step), y, c], (z_s, z_r), step - 1,
            device(x, y, lax.rem(z + step, NZ), c),
        )
        for step in (2, 6, 1, 7, 4, 3, 5)
    }
    load_index.wait()
    load_day.wait()
    days[0:DAY_DEV, :] = day_ref[...].astype(jnp.float32)
    days[DAY_DEV:DAY_ROWS, :] = jnp.zeros((DAY_ROWS - DAY_DEV, R), jnp.float32)
    meta[...] = jnp.zeros_like(meta)
    meta[0:3, :] = index_ref[...]
    meta[3:4, :] = jnp.full((1, CAP), live_ref[0], jnp.int32)
    swapped = [
        send(meta, meta_in, (m_s, m_r), 0, other),
        send(days.at[pl.ds(0, DAY_ROWS)], days.at[pl.ds(DAY_ROWS, DAY_ROWS)], (m_s, m_r), 1, other),
        send(
            counts_hbm.at[pl.ds(KEEP, CAP - KEEP)], counts.at[pl.ds(CAP, CAP - KEEP)],
            (m_s, m_r), 2, other,
        ),
    ]
    load_items.wait()
    item_sum = jnp.sum(items[...].astype(jnp.float32), axis=0, keepdims=True)
    day_sum = jnp.sum(day_ref[...].astype(jnp.float32), axis=0, keepdims=True)
    for part in range(R // 128):
        lanes = slice(part * 128, (part + 1) * 128)
        sums[part : part + 1, :] = item_sum[:, lanes]
        sums[part + 4 : part + 5, :] = day_sum[:, lanes]
    add = send(sums, sums_c, (tc_s, tc_r), 0, other)

    for step in (7, 1, 6, 2):
        along_z[step].wait()
    spread(0)
    add.wait()
    sums[...] += sums_c[...]
    adds = [
        send(sums, sums_b.at[step - 1], (tb_s, tb_r), step - 1, along(1 - c, me, step))
        for step in range(1, NX)
    ]
    for step in (5, 3, 4):
        along_z[step].wait()
    spread(1)
    for copy in adds:
        copy.wait()
    sums[...] += jnp.sum(sums_b[...], axis=0)
    adds = [
        send(sums, sums_a.at[step - 1], (ta_s, ta_r), step - 1, along(c, me, step))
        for step in range(1, NX)
    ]
    for share in (0, 1):
        for step in (1, 3, 2):
            along_a[step, share].wait()
            forward(step, share)
    for copy in adds:
        copy.wait()
    sums[...] += jnp.sum(sums_a[...], axis=0)
    adds = [
        send(sums, sums_z.at[step - 1], (tz_s, tz_r), step - 1, device(x, y, lax.rem(z + step, NZ), c))
        for step in (4, 3, 5, 2, 6, 1, 7)
    ]
    swapped[0].wait()
    first, second, groups = order_slots(meta[...], meta_in[...])
    plan[0:1, :] = first
    plan[1:2, :] = second
    plan[2:3, :] = groups
    plan[3:4, :] = user_places(z)
    plan[4:8, :] = jnp.zeros((4, CAP), jnp.int32)
    hand_plan = pltpu.make_async_copy(plan, plan_smem, local_sem.at[5])
    hand_plan.start()

    for back_a, share in ((0, 0), (0, 1), (1, 0), (3, 0), (2, 0), (1, 1), (3, 1), (2, 1)):
        for step in (1, 3, 2):
            along_b[step, back_a, share].wait()
            cross(back_a, step, share)
    for copy in adds:
        copy.wait()
    total_ref[...] = sums[...] + jnp.sum(sums_z[...], axis=0)
    swapped[1].wait()
    swapped[2].wait()
    load_counts.wait()
    hand_plan.wait()
    for copy in passed:
        copy.wait()


def gather_call(user_factors, item_factors, day_factors, tile_counts, tile_index, tile_live):
    dma = pltpu.SemaphoreType.DMA
    vmem = pl.BlockSpec(memory_space=pltpu.VMEM)
    hbm = pl.BlockSpec(memory_space=pltpu.HBM)
    tile = (8, 128)
    return pl.pallas_call(
        gather_kernel,
        out_shape=(
            pltpu.VMEM((NX, NZ, NY, NC, ROWS, R), jnp.bfloat16),
            pltpu.VMEM((ITEMBLK_DEV * TILE, R), jnp.bfloat16),
            pltpu.VMEM((2 * DAY_ROWS, R), jnp.float32),
            pltpu.VMEM((2 * CAP - KEEP, TILE, TILE), jnp.bfloat16),
            pltpu.SMEM(tile, jnp.int32),
            pltpu.VMEM(tile, jnp.float32),
        ),
        in_specs=[hbm] * 5 + [pl.BlockSpec(memory_space=pltpu.SMEM)],
        out_specs=(vmem,) * 4 + (pl.BlockSpec(memory_space=pltpu.SMEM), vmem),
        scratch_shapes=[
            pltpu.VMEM((ROWS, R), jnp.float32),
            pltpu.VMEM((DAY_DEV, R), jnp.bfloat16),
            pltpu.VMEM((3, CAP), jnp.int32),
            pltpu.VMEM(tile, jnp.int32),
            pltpu.VMEM(tile, jnp.int32),
            pltpu.VMEM(tile, jnp.int32),
            pltpu.VMEM(tile, jnp.float32),
            pltpu.VMEM(tile, jnp.float32),
            pltpu.VMEM((NX - 1,) + tile, jnp.float32),
            pltpu.VMEM((NX - 1,) + tile, jnp.float32),
            pltpu.VMEM((NZ - 1,) + tile, jnp.float32),
            dma((6,)),
        ]
        + [dma((NZ - 1,))] * 2 + [dma((NX - 1, 2))] * 2 + [dma((NX - 1, NX, 2))] * 2
        + [dma((NX, NX, 2))] * 2 + [dma((3,))] * 2
        + [dma((1,))] * 2 + [dma((NX - 1,))] * 4 + [dma((NZ - 1,))] * 2,
        compiler_params=pltpu.CompilerParams(
            collective_id=0, has_side_effects=True, vmem_limit_bytes=8 << 20
        ),
        name="gather_users",
    )(user_factors, item_factors, day_factors, tile_counts, tile_index, tile_live)


def phi_kernel(
    plan_ref, users_ref, item_ref, day_ref, counts_ref, phi_ref, w_even, w_odd, m_even, m_odd
):
    phi_ref[...] = jnp.zeros_like(phi_ref)
    groups = plan_ref[2, 0]

    def user_rows(block):
        return jnp.concatenate([users_ref[plan_ref[3, 2 * block + half]] for half in (0, 1)], axis=0)

    def codes(group):
        spot = FOUR * group
        row, col = lax.shift_right_logical(spot, 7), spot & (CAP - 1)
        return [plan_ref[row, col + part] for part in range(FOUR)]

    def user_block(code):
        return lax.shift_right_logical(jnp.maximum(code - 1, 0), 8) & (USER_BLOCKS - 1)

    def forward(group, w, m):
        group_codes = codes(group)
        for part, code in enumerate(group_codes):
            code = jnp.maximum(code - 1, 0)
            items = item_ref[lax.shift_right_logical(code, 12) & 3]
            scale = day_ref[pl.ds(lax.shift_right_logical(code, 14), 1), :]
            scale = jnp.broadcast_to(scale, (16, R)).astype(jnp.bfloat16)
            scaled = items.reshape(TILE // 16, 16, R) * scale[None]
            w[part * TILE : (part + 1) * TILE, :] = scaled.reshape(TILE, R)
        m[...] = lax.dot_general(
            user_rows(user_block(group_codes[0])), w[...], (((1,), (1,)), ((), ())),
            preferred_element_type=jnp.float32,
        )

    def backward(group, w, m):
        group_codes = codes(group)
        ratios = []
        for part, code in enumerate(group_codes):
            tile = counts_ref[jnp.maximum(code - 1, 0) & 255].astype(jnp.float32)
            ratio = tile / m[:, part * TILE : (part + 1) * TILE]
            ratios.append(jnp.where(code > 0, ratio, 0.0).astype(jnp.bfloat16))
        phi_ref[user_block(group_codes[0])] += jnp.dot(
            jnp.concatenate(ratios, axis=1), w[...], preferred_element_type=jnp.float32
        )

    forward(0, w_even, m_even)

    def turn(pair, carry):
        group = 2 * pair
        forward(group + 1, w_odd, m_odd)
        backward(group, w_even, m_even)
        forward(group + 2, w_even, m_even)
        backward(group + 1, w_odd, m_odd)
        return carry

    lax.fori_loop(0, lax.shift_right_logical(groups, 1), turn, 0)

    @pl.when((groups & 1) == 1)
    def _():
        backward(groups - 1, w_even, m_even)


def phi_call(plan, users, items, days, counts):
    vmem = pl.BlockSpec(memory_space=pltpu.VMEM)
    w = pltpu.VMEM((FOUR * TILE, R), jnp.bfloat16)
    m = pltpu.VMEM((TILE, FOUR * TILE), jnp.float32)
    return pl.pallas_call(
        phi_kernel,
        out_shape=pltpu.VMEM((USER_BLOCKS, TILE, R), jnp.float32),
        in_specs=[pl.BlockSpec(memory_space=pltpu.SMEM)] + [vmem] * 4,
        out_specs=vmem,
        scratch_shapes=[w, w, m, m],
        compiler_params=pltpu.CompilerParams(vmem_limit_bytes=32 << 20),
        name="tile_turns",
    )(plan, users, items, days, counts)


def scatter_kernel(
    phi_ref, user_ref, total_ref, out_ref,
    other, out_near, near, kept, out_far, far, deep,
    o_s, o_r, n_s, n_r, f_s, f_r, d_s, d_r,
):
    me = place()
    x, y, z, c = me
    p, q = pick(c, y, x), pick(c, x, y)
    greet(me)
    welcome()
    sibling = device(x, y, z, 1 - c)
    crossed, nears, fars = {}, {}, {}

    def cross(kq):
        for kp in STEPS:
            pp, qq = lax.rem(q + kp, NX), lax.rem(p + kq, NX)
            src = phi_ref.at[pick(c, pp, qq), :, pick(c, qq, pp), 1 - c]
            crossed[kp, kq] = send(src, other.at[kp, kq], (o_s, o_r), (kp, kq), sibling)

    cross(STEPS[0])
    for turn, kq in enumerate(STEPS):
        if turn + 1 < NX:
            cross(STEPS[turn + 1])
        for kp in STEPS:
            pp, qq = lax.rem(p + kp, NX), lax.rem(q + kq, NX)
            crossed[kp, kq].wait_recv()
            piece = phi_ref[pick(c, qq, pp), :, pick(c, pp, qq), c] + other[kp, kq]
            if kp:
                out_near[kp - 1, kq] = piece.reshape(NZ * ROWS, R).astype(jnp.bfloat16)
                nears[kp, kq] = send(
                    out_near.at[kp - 1, kq], near.at[kp - 1, kq], (n_s, n_r), (kp - 1, kq),
                    along(1 - c, me, kp),
                )
            else:
                kept[kq] = piece
    for kq in STEPS:
        piece = kept[kq]
        for kp in (1, 3, 2):
            nears[kp, kq].wait_recv()
            piece += near[kp - 1, kq].astype(jnp.float32).reshape(NZ, ROWS, R)
        if kq:
            out_far[kq - 1] = piece.reshape(NZ * ROWS, R).astype(jnp.bfloat16)
            fars[kq] = send(out_far.at[kq - 1], far.at[kq - 1], (f_s, f_r), kq - 1, along(c, me, kq))
        else:
            kept[0] = piece
    for kq in (1, 2, 3):
        fars[kq].wait_recv()
    arrived = jnp.sum(far[...].astype(jnp.float32), axis=0)
    kept[0] += arrived.reshape(NZ, ROWS, R)
    deeps = []
    for step in (4, 3, 5, 2, 6, 1, 7):
        there = lax.rem(z + step, NZ)
        deeps.append(
            send(kept.at[0, there], deep.at[step - 1], (d_s, d_r), step - 1,
                 device(x, y, there, c))
        )
    totals = total_ref[0:4, :] * total_ref[4:8, :] * (1.0 / (NX * NZ * NY * NC))
    for copy in deeps:
        copy.wait_recv()
    summed = kept[0, z] + jnp.sum(deep[...], axis=0)
    for part in range(R // 128):
        lanes = slice(part * 128, (part + 1) * 128)
        out_ref[:, lanes] = user_ref[:, lanes] * summed[:, lanes] / totals[part : part + 1, :]
    for group in (crossed.values(), nears.values(), fars.values(), deeps):
        for copy in group:
            copy.wait_send()


def scatter_call(phi, user_factors, totals):
    dma = pltpu.SemaphoreType.DMA
    vmem = pl.BlockSpec(memory_space=pltpu.VMEM)
    piece = (NZ, ROWS, R)
    return pl.pallas_call(
        scatter_kernel,
        out_shape=jax.ShapeDtypeStruct((ROWS, R), jnp.float32),
        in_specs=[vmem] * 3,
        out_specs=vmem,
        scratch_shapes=[
            pltpu.VMEM((NX, NX) + piece, jnp.float32),
            pltpu.VMEM((NX - 1, NX, NZ * ROWS, R), jnp.bfloat16),
            pltpu.VMEM((NX - 1, NX, NZ * ROWS, R), jnp.bfloat16),
            pltpu.VMEM((NX,) + piece, jnp.float32),
            pltpu.VMEM((NX - 1, NZ * ROWS, R), jnp.bfloat16),
            pltpu.VMEM((NX - 1, NZ * ROWS, R), jnp.bfloat16),
            pltpu.VMEM((NZ - 1, ROWS, R), jnp.float32),
            dma((NX, NX)), dma((NX, NX)),
            dma((NX - 1, NX)), dma((NX - 1, NX)),
            dma((NX - 1,)), dma((NX - 1,)),
            dma((NZ - 1,)), dma((NZ - 1,)),
        ],
        compiler_params=pltpu.CompilerParams(
            collective_id=1, has_side_effects=True, vmem_limit_bytes=24 << 20
        ),
        name="sum_phi",
    )(phi, user_factors, totals)


def per_device(user_factors, item_factors, day_factors, tile_counts, tile_index, tile_live):
    in_hbm = functools.partial(pltpu.with_memory_space_constraint, memory_space=pltpu.HBM)
    users, items, days, counts, plan, totals = gather_call(
        *map(in_hbm, (user_factors, item_factors, day_factors, tile_counts, tile_index)), tile_live
    )
    phi = phi_call(
        plan, users.reshape(NX * NZ, TILE // 2, R), items.reshape(ITEMBLK_DEV, TILE, R), days, counts
    )
    return scatter_call(phi.reshape(NX, NZ, NY, NC, ROWS, R), user_factors, totals)


def solution(mesh):
    in_specs = (
        P(("item", "day"), None),
        P("item", None),
        P("day", None),
        P(("item", "day"), None, None),
        P(None, ("item", "day")),
        P(("item", "day")),
    )
    out_specs = P(("item", "day"), None)
    return jax.shard_map(
        per_device, mesh=mesh, in_specs=in_specs, out_specs=out_specs, check_vma=False
    )
```
